32 devices in a mesh: wide: 8 (over y, x, core), narrow: 4 (over z).
Axes of the slice: x: 2, y: 2, z: 4, core: 2. Of those that a mesh axis runs over, the one named last changes fastest.
Arguments:
- tokens: bfloat16 [32, 512, 256], P('wide', 'narrow'), may hold values from -6 to 6
- kind: int32 [32], P('wide'), may hold values from 0 to 1
- proj_weight: bfloat16 [2, 256, 768], replicated, may hold values from -0.375 to 0.375
- proj_bias: float32 [2, 768], replicated, may hold values from -1.8 to 1.8
- ln1_gain: float32 [768], replicated, may hold values from 0.5 to 1.5
- ln1_bias: float32 [768], replicated, may hold values from -1.2 to 1.2
- qkv_weight: bfloat16 [768, 3, 768], P(None, None, 'narrow'), may hold values from -0.21875 to 0.21875
- qv_bias: float32 [2, 768], P(None, 'narrow'), may hold values from -1.8 to 1.8
- out_weight: bfloat16 [768, 768], P('narrow'), may hold values from -0.75 to 0.75
- out_bias: float32 [768], replicated, may hold values from -1.2 to 1.2
- ln2_gain: float32 [768], replicated, may hold values from 0.5 to 1.5
- ln2_bias: float32 [768], replicated, may hold values from -1.2 to 1.2
- up_weight: bfloat16 [768, 3072], P(None, 'narrow'), may hold values from -0.21875 to 0.21875
- up_bias: float32 [3072], replicated, may hold values from -1.8 to 1.8
- down_weight: bfloat16 [3072, 768], P('narrow'), may hold values from -0.109375 to 0.109375
- down_bias: float32 [768], replicated, may hold values from -1.2 to 1.2
- cotangent: bfloat16 [32, 512, 768], P('wide', 'narrow'), may hold values from -6 to 6
Outputs:
- out: bfloat16 [32, 512, 768], P('wide', 'narrow')
- tokens_grad: float32 [32, 512, 256], P('wide', 'narrow')
- proj_weight_grad: float32 [2, 256, 768], replicated
- proj_bias_grad: float32 [2, 768], replicated
- ln1_gain_grad: float32 [768], replicated
- ln1_bias_grad: float32 [768], replicated
- qkv_weight_grad: float32 [768, 3, 768], P(None, None, 'narrow')
- qv_bias_grad: float32 [2, 768], P(None, 'narrow')
- out_weight_grad: float32 [768, 768], P('narrow')
- out_bias_grad: float32 [768], replicated
- ln2_gain_grad: float32 [768], replicated
- ln2_bias_grad: float32 [768], replicated
- up_weight_grad: float32 [768, 3072], P(None, 'narrow')
- up_bias_grad: float32 [3072], P('narrow')
- down_weight_grad: float32 [3072, 768], P('narrow')
- down_bias_grad: float32 [768], replicated
The draws below stay inside these ranges and needn't reach their ends.
Inputs may be any that keep to these rules, and one draw needn't show every extreme that they name: kind[c] is 0 for a clip of frame tokens and 1 for a clip of patch tokens.
All inputs are finite; a program needn't handle non-finite values.
Results may differ from the reference program's by a relative error of at most 0.019.
Values may be sent and summed in bfloat16 or wider, within the bound.
No kernel may reach another device: no remote copies, remote signals or barrier semaphores. Data moves between devices by JAX's collectives and lax.ppermute only.
A program may use at most 192 MiB of HBM per device.

```python
import math
import jax
import jax.numpy as jnp
from jax import lax

D = 768
HEADS = 12
HEAD_DIM = 64
FF = 3072
FEAT = 256
SEQ = 512
CLIPS = 32


def plant(entries, own_key, low, high):
    longest = entries.shape.index(max(entries.shape))
    spots = []
    for shift in (0, 1):
        where = [jax.random.randint(jax.random.fold_in(own_key, axis), (), 0, length) for axis, length in enumerate(entries.shape)]
        where[longest] = (where[longest] + shift) % entries.shape[longest]
        spots.append(tuple(where))
    return entries.at[spots[0]].set(low).at[spots[1]].set(high)


def shard_levels(rng, shape, split, smallest, high):
    def one(position, shards_of):
        steps = jax.random.uniform(jax.random.fold_in(jax.random.fold_in(rng, 6), position), (shards_of,), jnp.float32, smallest / len(split), high / len(split))
        return jnp.repeat(jnp.exp(steps), shape[position] // shards_of).reshape((-1,) + (1,) * (len(shape) - position - 1))

    gain = one(*split[0])
    for cut in split[1:]:
        gain = gain * one(*cut)
    return gain


def scatter_about(own_key, extent, scale, bound, cuts=(), kind=jnp.bfloat16):
    loudness = shard_levels(own_key, extent, cuts, -0.22, 0.18) if cuts else 1.0
    values = jax.random.normal(own_key, extent, jnp.float32) * scale * loudness
    return jnp.minimum(jnp.maximum(values, -bound), bound).astype(kind)


def setup_inputs(seed: int = 0) -> dict:
    seeds = jax.random.split(jax.random.key(seed), 18)
    return {
        "tokens": scatter_about(seeds[0], (CLIPS, SEQ, FEAT), 1.0, 6.0, ((0, 8), (1, 4))),
        "kind": plant(jax.random.randint(seeds[1], (CLIPS,), 0, 2), jax.random.fold_in(seeds[1], 1), 0, 1).astype(jnp.int32),
        "proj_weight": scatter_about(seeds[2], (2, FEAT, D), FEAT ** -0.5, 0.375),
        "proj_bias": scatter_about(seeds[3], (2, D), 0.3, 1.8, (), jnp.float32),
        "ln1_gain": jnp.clip(1.0 + 0.1 * jax.random.normal(seeds[4], (D,), jnp.float32), 0.5, 1.5),
        "ln1_bias": scatter_about(seeds[5], (D,), 0.2, 1.2, (), jnp.float32),
        "qkv_weight": scatter_about(seeds[6], (D, 3, D), D ** -0.5, 0.21875, ((2, 4),)),
        "qv_bias": scatter_about(seeds[7], (2, D), 0.3, 1.8, ((1, 4),), jnp.float32),
        "out_weight": scatter_about(seeds[8], (D, D), HEAD_DIM ** -0.5, 0.75, ((0, 4),)),
        "out_bias": scatter_about(seeds[9], (D,), 0.2, 1.2, (), jnp.float32),
        "ln2_gain": jnp.clip(1.0 + 0.1 * jax.random.normal(seeds[10], (D,), jnp.float32), 0.5, 1.5),
        "ln2_bias": scatter_about(seeds[11], (D,), 0.2, 1.2, (), jnp.float32),
        "up_weight": scatter_about(seeds[12], (D, FF), D ** -0.5, 0.21875, ((1, 4),)),
        "up_bias": scatter_about(seeds[13], (FF,), 0.3, 1.8, (), jnp.float32),
        "down_weight": scatter_about(seeds[14], (FF, D), FF ** -0.5, 0.109375, ((0, 4),)),
        "down_bias": scatter_about(seeds[15], (D,), 0.2, 1.2, (), jnp.float32),
        "cotangent": scatter_about(seeds[16], (CLIPS, SEQ, D), 1.0, 6.0, ((0, 8), (1, 4))),
    }


@jax.custom_vjp
def low(v):
    return lax.optimization_barrier(v.astype(jnp.bfloat16)).astype(jnp.float32)

@jax.custom_vjp
def low_back(v):
    return v

def low_keep(v):
    return (low(v), None)

def low_pass(kept, grad):
    return (grad,)

def back_keep(v):
    return (v, None)

def back_low(kept, grad):
    return (low(grad),)
low.defvjp(low_keep, low_pass)
low_back.defvjp(back_keep, back_low)
epsilon = 1e-06
precise = lax.Precision.HIGHEST

def layer_norm(values, norm_gain, norm_shift):
    row_mean = lax.optimization_barrier(jnp.mean(values, axis=-1, keepdims=True))
    centred = values - row_mean
    row_var = lax.optimization_barrier(jnp.mean(centred * centred, axis=-1, keepdims=True))
    return centred * lax.rsqrt(row_var + epsilon) * norm_gain + norm_shift

def exact_gelu(values):
    return 0.5 * values * (1.0 + jax.scipy.special.erf(values * 2.0 ** (-0.5)))

def encoder_block(params, clip_tokens, clip_kinds):
    proj_weight, proj_bias, ln1_gain, ln1_bias, qkv_weight, qv_bias, out_weight, out_bias, ln2_gain, ln2_bias, up_weight, up_bias, down_weight, down_bias = params
    batch_clips = clip_tokens.shape[0]
    chosen = jnp.einsum('bk,kfd->bfd', clip_kinds, proj_weight, precision=precise)
    chosen_bias = jnp.einsum('bk,kd->bd', clip_kinds, proj_bias, precision=precise)
    start_rows = low_back(jnp.einsum('blf,bfd->bld', clip_tokens, chosen, precision=precise) + chosen_bias[:, None, :])
    normed_one = low(layer_norm(start_rows, ln1_gain, ln1_bias))
    queries = low(low_back(jnp.einsum('bld,de->ble', normed_one, qkv_weight[:, 0], precision=precise) + qv_bias[0]))
    keys_all = low(low_back(jnp.einsum('bld,de->ble', normed_one, qkv_weight[:, 1], precision=precise)))
    values_all = low(low_back(jnp.einsum('bld,de->ble', normed_one, qkv_weight[:, 2], precision=precise) + qv_bias[1]))
    head_shape = (batch_clips, SEQ, HEADS, HEAD_DIM)
    scores = low_back(jnp.einsum('blhe,bmhe->bhlm', queries.reshape(head_shape), keys_all.reshape(head_shape), precision=precise) * HEAD_DIM ** (-0.5))
    shifted = jnp.exp(scores - lax.optimization_barrier(jnp.max(scores, axis=-1, keepdims=True)))
    weights = low(shifted / lax.optimization_barrier(jnp.sum(shifted, axis=-1, keepdims=True)))
    mixed = low(low_back(jnp.einsum('bhlm,bmhe->blhe', weights, values_all.reshape(head_shape), precision=precise).reshape(batch_clips, SEQ, D)))
    middle = start_rows + low_back(jnp.einsum('ble,ed->bld', mixed, out_weight, precision=precise) + out_bias)
    normed_two = low(layer_norm(middle, ln2_gain, ln2_bias))
    hidden_pre = low_back(jnp.einsum('bld,df->blf', normed_two, up_weight, precision=precise) + up_bias)
    hidden = low(exact_gelu(hidden_pre))
    return middle + low_back(jnp.einsum('blf,fd->bld', hidden, down_weight, precision=precise) + down_bias)

def reference(tokens, kind, proj_weight, proj_bias, ln1_gain, ln1_bias, qkv_weight, qv_bias, out_weight, out_bias, ln2_gain, ln2_bias, up_weight, up_bias, down_weight, down_bias, cotangent):
    params = tuple((array_in.astype(jnp.float32) for array_in in (proj_weight, proj_bias, ln1_gain, ln1_bias, qkv_weight, qv_bias, out_weight, out_bias, ln2_gain, ln2_bias, up_weight, up_bias, down_weight, down_bias)))
    block_clips = math.gcd(CLIPS, max(1, 4096 // SEQ))
    num_blocks = CLIPS // block_clips
    clip_kinds = jax.nn.one_hot(kind, 2, dtype=jnp.float32).reshape(num_blocks, block_clips, 2)
    token_blocks = tokens.astype(jnp.float32).reshape(num_blocks, block_clips, SEQ, FEAT)

    def forward(weights_in, blocks_in):

        def one_block(block_pair):
            return encoder_block(weights_in, block_pair[0], block_pair[1])
        return lax.map(jax.checkpoint(one_block), (blocks_in, clip_kinds))
    final_rows, pullback = jax.vjp(forward, params, token_blocks)
    param_grads, token_grads = pullback(cotangent.astype(jnp.float32).reshape(num_blocks, block_clips, SEQ, D))
    return (final_rows.reshape(CLIPS, SEQ, D).astype(jnp.bfloat16), token_grads.reshape(CLIPS, SEQ, FEAT), param_grads[0], param_grads[1], param_grads[2], param_grads[3], param_grads[4], param_grads[5], param_grads[6], param_grads[7], param_grads[8], param_grads[9], param_grads[10], param_grads[11], param_grads[12], param_grads[13])
```

```python
import functools

import jax
import jax.numpy as jnp
from jax import lax
from jax.experimental import pallas as pl
from jax.experimental.pallas import tpu as pltpu
from jax.sharding import PartitionSpec as P

HEAD_DIM = 64
SCALE = HEAD_DIM ** (-0.5)
EPS = 1e-06
F32 = jnp.float32
BF16 = jnp.bfloat16
NN = (((1,), (0,)), ((), ()))
NT = (((1,), (1,)), ((), ()))
TN = (((0,), (0,)), ((), ()))


def dot(a, b, dims):
    return lax.dot_general(a, b, dims, preferred_element_type=F32)


def row_stats(v):
    mean = jnp.mean(v, axis=-1, keepdims=True)
    cen = v - mean
    var = jnp.mean(cen * cen, axis=-1, keepdims=True)
    return cen, lax.rsqrt(var + EPS)


def norm_back(v, grad, gain):
    cen, r = row_stats(v)
    xhat = cen * r
    q = grad * gain
    mq = jnp.mean(q, axis=-1, keepdims=True)
    mqx = jnp.mean(q * xhat, axis=-1, keepdims=True)
    return r * (q - mq - xhat * mqx), xhat


def gelu_pair(u):
    phi = 0.5 * (1.0 + lax.erf(u * (2.0 ** -0.5)))
    dens = jnp.exp(-0.5 * u * u) * 0.3989422804014327
    return u * phi, phi + u * dens


def attn_fwd_kernel(kind, x, proj, pbias, g1, b1, wq, bq, wo, ob, g2, b2,
                    start, n1, qkv, mixed, lse, middle, n2):
    z = pl.program_id(0)
    nz = pl.num_programs(0)

    @pl.when(z == 0)
    def _():
        s = dot(x[...], proj[0], NN) + pbias[0]
        start[...] = s
        middle[...] = s + ob[...]
        cen, r = row_stats(s)
        n1[...] = (cen * r * g1[...] + b1[...]).astype(BF16)

    qkv[0] = (dot(wq[0], n1[...], NT) + bq[0]).astype(BF16)
    width = mixed.shape[1]
    for h in range(width // HEAD_DIM):
        lo = h * HEAD_DIM
        q_t = qkv[0, lo:lo + HEAD_DIM, :]
        k_t = qkv[0, width + lo:width + lo + HEAD_DIM, :]
        v_t = qkv[0, 2 * width + lo:2 * width + lo + HEAD_DIM, :]
        s = dot(k_t, q_t, TN) * SCALE
        top = jnp.max(s, axis=0, keepdims=True)
        e = jnp.exp(s - top)
        total = jnp.sum(e, axis=0, keepdims=True)
        p = (e * (1.0 / total)).astype(BF16)
        lse[0, h:h + 1, :] = top + jnp.log(total)
        mixed[0, lo:lo + HEAD_DIM, :] = dot(v_t, p, NN).astype(BF16)
    middle[...] += dot(mixed[0], wo[0], TN)

    @pl.when(z == nz - 1)
    def _():
        cen, r = row_stats(middle[...])
        n2[...] = (cen * r * g2[...] + b2[...]).astype(BF16)


def ffn_kernel(n2, g, middle, up, ub, down, db, g2,
               out, mid_grad, mid_low, dup, ddown, dub, sums, acc, dn2, n2t):
    z = pl.program_id(0)
    nz = pl.num_programs(0)

    @pl.when(z == 0)
    def _():
        acc[...] = middle[...] + db[...]
        dn2[...] = jnp.zeros_like(dn2)
        n2t[...] = n2[...].T

    u = dot(n2[...], up[0], NN) + ub[0]
    h, slope = gelu_pair(u)
    h = h.astype(BF16)
    acc[...] += dot(h, down[0], NN)
    ddown[0] = dot(h, g[...], TN).astype(BF16)
    pre = (dot(g[...], down[0], NT) * slope).astype(BF16)
    dub[0] = jnp.sum(pre.astype(F32), axis=0, keepdims=True)
    dup[0] = dot(n2t[...], pre, NN).astype(BF16)
    dn2[...] += dot(pre, up[0], NT)

    @pl.when(z == nz - 1)
    def _():
        out[...] = acc[...].astype(BF16)
        gf = g[...].astype(F32)
        d = dn2[...]
        back, xhat = norm_back(middle[...], d, g2[...])
        mg = gf + back
        mid_grad[...] = mg
        ml = mg.astype(BF16)
        mid_low[...] = ml
        sums[...] = jnp.concatenate([
            jnp.sum(d * xhat, axis=0, keepdims=True),
            jnp.sum(d, axis=0, keepdims=True),
            jnp.sum(ml.astype(F32), axis=0, keepdims=True),
            jnp.sum(gf, axis=0, keepdims=True),
        ], axis=0)


def attn_bwd_kernel(kind, mid_low, mid_grad, start, n1, x, proj, g1, wq, wo, qkv, mixed, lse,
                    dqkv_w, dout_w, dqv, tok_grad, dproj, sums, dn1, dqkv):
    z = pl.program_id(0)
    nz = pl.num_programs(0)

    @pl.when(z == 0)
    def _():
        dn1[...] = jnp.zeros_like(dn1)

    ml = mid_low[...]
    dout_w[0] = dot(mixed[0], ml, NN).astype(BF16)
    do_all = dot(wo[0], ml, NT).astype(BF16)
    width = mixed.shape[1]
    for h in range(width // HEAD_DIM):
        lo = h * HEAD_DIM
        q_t = qkv[0, lo:lo + HEAD_DIM, :]
        k_t = qkv[0, width + lo:width + lo + HEAD_DIM, :]
        v_t = qkv[0, 2 * width + lo:2 * width + lo + HEAD_DIM, :]
        do_t = do_all[lo:lo + HEAD_DIM, :]
        p = jnp.exp(dot(k_t, q_t, TN) * SCALE - lse[0, h:h + 1, :])
        dp = dot(v_t, do_t, TN)
        dsum = jnp.sum(p * dp, axis=0, keepdims=True)
        ds = (p * (dp - dsum)).astype(BF16)
        dqkv[lo:lo + HEAD_DIM, :] = (dot(k_t, ds, NN) * SCALE).astype(BF16)
        dqkv[width + lo:width + lo + HEAD_DIM, :] = (dot(q_t, ds, NT) * SCALE).astype(BF16)
        dqkv[2 * width + lo:2 * width + lo + HEAD_DIM, :] = dot(do_t, p.astype(BF16), NT).astype(BF16)
    dw = dqkv[...]
    dqv[0] = jnp.sum(dw.astype(F32), axis=1, keepdims=True)
    dqkv_w[0] = dot(dw, n1[...], NN).astype(BF16)
    dn1[...] += dot(dw, wq[0], TN)

    @pl.when(z == nz - 1)
    def _():
        d = dn1[...]
        back, xhat = norm_back(start[...], d, g1[...])
        sl = (mid_grad[...] + back).astype(BF16)
        tok_grad[...] = dot(sl, proj[0], NT).astype(tok_grad.dtype)
        dproj[...] = dot(x[...], sl, TN)
        sums[...] = jnp.concatenate([
            jnp.sum(sl.astype(F32), axis=0, keepdims=True),
            jnp.sum(d * xhat, axis=0, keepdims=True),
            jnp.sum(d, axis=0, keepdims=True),
            jnp.zeros_like(g1[...]),
        ], axis=0)


def whole(shape):
    return pl.BlockSpec(shape, lambda z, *_: (0,) * len(shape))


def part(shape):
    return pl.BlockSpec((1,) + shape, lambda z, *_: (z,) + (0,) * len(shape))


def by_kind(shape):
    return pl.BlockSpec((1,) + shape, lambda z, k: (k[0],) + (0,) * len(shape))


def sds(shape, dtype):
    return jax.ShapeDtypeStruct(shape, dtype)


PARAMS = pltpu.CompilerParams(dimension_semantics=("arbitrary",), vmem_limit_bytes=56 << 20)


def attn_fwd(kind, x, proj, pbias, g1, b1, wq, bq, wo, ob, g2, b2):
    nz, qw, d = wq.shape
    hw = wo.shape[1]
    seq, feat = x.shape
    row = (1, d)
    return pl.pallas_call(
        attn_fwd_kernel,
        grid_spec=pltpu.PrefetchScalarGridSpec(
            num_scalar_prefetch=1, grid=(nz,),
            in_specs=[whole((seq, feat)), by_kind((feat, d)), by_kind(row), whole(row), whole(row),
                      part((qw, d)), part((qw, 1)), part((hw, d)), whole(row), whole(row), whole(row)],
            out_specs=[whole((seq, d)), whole((seq, d)), part((qw, seq)), part((hw, seq)),
                       part((8, seq)), whole((seq, d)), whole((seq, d))]),
        out_shape=[sds((seq, d), F32), sds((seq, d), BF16), sds((nz, qw, seq), BF16),
                   sds((nz, hw, seq), BF16), sds((nz, 8, seq), F32), sds((seq, d), F32),
                   sds((seq, d), BF16)],
        compiler_params=PARAMS, name="attn_fwd",
    )(kind, x, proj, pbias, g1, b1, wq, bq, wo, ob, g2, b2)


def ffn(n2, g, middle, up, ub, down, db, g2):
    nz, d, f = up.shape
    seq = n2.shape[0]
    row = (1, d)
    return pl.pallas_call(
        ffn_kernel,
        grid_spec=pltpu.PrefetchScalarGridSpec(
            num_scalar_prefetch=0, grid=(nz,),
            in_specs=[whole((seq, d)), whole((seq, d)), whole((seq, d)), part((d, f)), part((1, f)),
                      part((f, d)), whole(row), whole(row)],
            out_specs=[whole((seq, d)), whole((seq, d)), whole((seq, d)), part((d, f)), part((f, d)),
                       part((1, f)), whole((4, d))],
            scratch_shapes=[pltpu.VMEM((seq, d), F32), pltpu.VMEM((seq, d), F32),
                            pltpu.VMEM((d, seq), BF16)]),
        out_shape=[sds((seq, d), BF16), sds((seq, d), F32), sds((seq, d), BF16), sds((nz, d, f), BF16),
                   sds((nz, f, d), BF16), sds((nz, 1, f), F32), sds((4, d), F32)],
        compiler_params=PARAMS, name="ffn",
    )(n2, g, middle, up, ub, down, db, g2)


def attn_bwd(kind, mid_low, mid_grad, start, n1, x, proj, g1, wq, wo, qkv, mixed, lse):
    nz, qw, d = wq.shape
    hw = wo.shape[1]
    seq, feat = x.shape
    row = (1, d)
    return pl.pallas_call(
        attn_bwd_kernel,
        grid_spec=pltpu.PrefetchScalarGridSpec(
            num_scalar_prefetch=1, grid=(nz,),
            in_specs=[whole((seq, d)), whole((seq, d)), whole((seq, d)), whole((seq, d)),
                      whole((seq, feat)), by_kind((feat, d)), whole(row), part((qw, d)), part((hw, d)),
                      part((qw, seq)), part((hw, seq)), part((8, seq))],
            out_specs=[part((qw, d)), part((hw, d)), part((qw, 1)), whole((seq, feat)),
                       whole((feat, d)), whole((4, d))],
            scratch_shapes=[pltpu.VMEM((seq, d), F32), pltpu.VMEM((qw, seq), BF16)]),
        out_shape=[sds((nz, qw, d), BF16), sds((nz, hw, d), BF16), sds((nz, qw, 1), F32),
                   sds((seq, feat), BF16), sds((feat, d), F32), sds((4, d), F32)],
        compiler_params=PARAMS, name="attn_bwd",
    )(kind, mid_low, mid_grad, start, n1, x, proj, g1, wq, wo, qkv, mixed, lse)


def per_device(nw, nz, tokens, kind, proj_weight, proj_bias, ln1_gain, ln1_bias, qkv_weight, qv_bias,
               out_weight, out_bias, ln2_gain, ln2_bias, up_weight, up_bias, down_weight, down_bias,
               cotangent):
    me_w = lax.axis_index("wide")
    me_z = lax.axis_index("narrow")
    d = up_weight.shape[0]
    hw = out_weight.shape[0]

    def gather(shard):
        rows = shard.shape[0]
        mine = lax.dynamic_slice_in_dim(shard, me_w * (rows // nw), rows // nw, 0)
        full = lax.all_gather(mine, ("narrow", "wide"), axis=0, tiled=True)
        return full.reshape((nz, rows) + shard.shape[1:])

    def reduce(grad):
        rows = grad.shape[1]
        flat = grad.reshape((nz * rows,) + grad.shape[2:])
        mine = lax.psum_scatter(flat, ("narrow", "wide"), scatter_dimension=0, tiled=True)
        return lax.all_gather(mine, "wide", axis=0, tiled=True).astype(F32)

    def to_clip(v):
        return lax.all_to_all(v, "narrow", 0, 1, tiled=True)[0]

    def to_rows(v):
        return lax.all_to_all(v[None], "narrow", 1, 0, tiled=True)

    x = to_clip(tokens)
    wq = gather(jnp.transpose(qkv_weight, (1, 2, 0)).reshape(3 * hw, d))
    wo = gather(out_weight)
    up = gather(up_weight)
    down = gather(down_weight)
    g = to_clip(cotangent)
    zero_row = jnp.zeros_like(qv_bias[0])
    bias_three = jnp.concatenate([qv_bias[0], zero_row, qv_bias[1]])
    bq = lax.all_gather(bias_three, "narrow", axis=0)[:, :, None]
    ub = up_bias.reshape(nz, 1, d)
    my_kind = lax.dynamic_slice_in_dim(kind, me_z, 1, 0)
    my_kind = jnp.where(my_kind == 1, 1, 0).astype(jnp.int32)
    r = lambda v: v.reshape(1, d)

    start, n1, qkv, mixed, lse, middle, n2 = attn_fwd(
        my_kind, x, proj_weight, proj_bias[:, None, :], r(ln1_gain), r(ln1_bias), wq, bq, wo,
        r(out_bias), r(ln2_gain), r(ln2_bias))
    out, mid_grad, mid_low, dup, ddown, dub, sums2 = ffn(
        n2, g, middle, up, ub, down, r(down_bias), r(ln2_gain))
    dqkv_w, dout_w, dqv, tok_grad, dproj, sums1 = attn_bwd(
        my_kind, mid_low, mid_grad, start, n1, x, proj_weight, r(ln1_gain), wq, wo, qkv, mixed, lse)

    output = to_rows(out)
    tokens_grad = to_rows(tok_grad).astype(F32)
    dup_s = reduce(dup)
    ddown_s = reduce(ddown)
    dqkv_s = reduce(dqkv_w)
    dout_s = reduce(dout_w)
    is_patch = my_kind[0] == 1
    proj_pair = jnp.stack([jnp.where(is_patch, 0.0, dproj), jnp.where(is_patch, dproj, 0.0)])
    bias_pair = jnp.stack([jnp.where(is_patch, 0.0, sums1[0]), jnp.where(is_patch, sums1[0], 0.0)])
    dqv_cols = dqv.reshape(nz, 3, hw)
    small = jnp.concatenate([
        bias_pair, sums1[1:3], sums2, dub.reshape(nz, d),
        dqv_cols[:, 0].reshape(1, -1), dqv_cols[:, 2].reshape(1, -1)], axis=0)
    proj_sum = lax.psum(proj_pair.astype(BF16), ("wide", "narrow")).astype(F32)
    small = lax.psum(small, ("wide", "narrow"))
    up_b = lax.dynamic_index_in_dim(small, 8 + me_z, 0, keepdims=False)
    qv = lax.dynamic_slice_in_dim(small[8 + nz:10 + nz], me_z * hw, hw, 1)
    qkv_sum = jnp.transpose(dqkv_s.reshape(3, hw, d), (2, 0, 1))
    return (output, tokens_grad, proj_sum, small[0:2], small[2], small[3], qkv_sum, qv, dout_s,
            small[6], small[4], small[5], dup_s, up_b, ddown_s, small[7])


def solution(mesh):
    in_specs = (
        P("wide", "narrow", None), P("wide"), P(), P(), P(), P(), P(None, None, "narrow"),
        P(None, "narrow"), P("narrow", None), P(), P(), P(), P(None, "narrow"), P(),
        P("narrow", None), P(), P("wide", "narrow", None),
    )
    out_specs = (
        P("wide", "narrow", None), P("wide", "narrow", None), P(), P(), P(), P(),
        P(None, None, "narrow"), P(None, "narrow"), P("narrow", None), P(), P(), P(),
        P(None, "narrow"), P("narrow"), P("narrow", None), P(),
    )
    body = functools.partial(per_device, mesh.shape["wide"], mesh.shape["narrow"])
    return jax.shard_map(
        body, mesh=mesh, in_specs=in_specs, out_specs=out_specs, check_vma=False
    )
```

```python
import functools

import jax
import jax.numpy as jnp
from jax import lax
from jax.experimental import pallas as pl
from jax.experimental.pallas import tpu as pltpu
from jax.sharding import PartitionSpec as P

HEAD_DIM = 64
SCALE = HEAD_DIM ** (-0.5)
EPS = 1e-06
F32 = jnp.float32
BF16 = jnp.bfloat16
NN = (((1,), (0,)), ((), ()))
NT = (((1,), (1,)), ((), ()))
TN = (((0,), (0,)), ((), ()))


def dot(a, b, dims):
    return lax.dot_general(a, b, dims, preferred_element_type=F32)


def row_stats(v):
    mean = jnp.mean(v, axis=-1, keepdims=True)
    cen = v - mean
    var = jnp.mean(cen * cen, axis=-1, keepdims=True)
    return cen, lax.rsqrt(var + EPS)


def norm_back(v, grad, gain):
    cen, r = row_stats(v)
    xhat = cen * r
    q = grad * gain
    mq = jnp.mean(q, axis=-1, keepdims=True)
    mqx = jnp.mean(q * xhat, axis=-1, keepdims=True)
    return r * (q - mq - xhat * mqx), xhat


def gelu_pair(u):
    phi = 0.5 * (1.0 + lax.erf(u * (2.0 ** -0.5)))
    dens = jnp.exp(-0.5 * u * u) * 0.3989422804014327
    return u * phi, phi + u * dens


def rows_of(i, size):
    start = i * size
    return pl.ds(pl.multiple_of(start, size & -size), size)


def step_bits(n, flip):
    bits = [1 << k for k in range(1, n.bit_length() - 1)]
    return bits[::-1] if flip else bits


def kept(n, flip):
    order = [0]
    for b in step_bits(n, flip)[::-1]:
        order = order + [r | b for r in order]
    return order


def spread_order(n, flip):
    bits = step_bits(n, flip)[::-1]
    sets = [[0]]
    for b in bits:
        now = [r for one in sets for r in one]
        sets = [now, [r ^ b for r in now]]
    return sets + [[r ^ 1 for r in one] for one in sets]


def put_pieces(dst, base, bufs, me, n, flip):
    for ref, rs in zip(bufs, spread_order(n, flip)):
        size = ref.shape[2]
        for i, r in enumerate(rs):
            dst[rows_of(base // size + (me ^ r), size), :] = ref[i, 0]


def cut_pieces(src, base, keep, send, me, n, flip, size, at=None):
    for i, r in enumerate(kept(n, flip)):
        for ref, q in ((keep, r), (send, r | 1)):
            val = src[rows_of(base // size + (me ^ q), size), :]
            if at is None:
                ref[i, 0] = val
            else:
                ref[i, at, 0:size] = val


def attn_fwd_kernel(n, nbuf, idx, *refs):
    xs, refs = refs[:nbuf[0]], refs[nbuf[0]:]
    proj, pbias, g1, b1, own_a, own_b, bq, ob, g2, b2 = refs[:10]
    refs = refs[10:]
    pa, pb, refs = refs[:nbuf[1]], refs[nbuf[1]:2 * nbuf[1]], refs[2 * nbuf[1]:]
    start, n1, qkv, mixed, lse, middle, n2, w, xfull = refs
    z = pl.program_id(0)
    nz = pl.num_programs(0)
    me = idx[1]
    half = own_a.shape[0]

    @pl.when(z == 0)
    def _():
        part_rows = xs[0].shape[0]
        for s, ref in enumerate(xs):
            xfull[rows_of(lax.rem(idx[2] - s + len(xs), len(xs)), part_rows), :] = ref[...]
        s = dot(xfull[...], proj[0], NN) + pbias[0]
        start[...] = s
        middle[...] = s + ob[...]
        cen, r = row_stats(s)
        n1[...] = (cen * r * g1[...] + b1[...]).astype(BF16)
        w[0, 0:half, :] = own_a[...]
        w[0, half:2 * half, :] = own_b[...]

    @pl.when(z > 0)
    def _():
        put_pieces(w.at[0], 0, pa, me, n, False)
        put_pieces(w.at[0], half, pb, me, n, True)

    width = mixed.shape[1]
    qkv[0] = (dot(w[0, 0:3 * width, :], n1[...], NT) + bq[0]).astype(BF16)
    for h in range(width // HEAD_DIM):
        lo = h * HEAD_DIM
        q_t = qkv[0, lo:lo + HEAD_DIM, :]
        k_t = qkv[0, width + lo:width + lo + HEAD_DIM, :]
        v_t = qkv[0, 2 * width + lo:2 * width + lo + HEAD_DIM, :]
        s = dot(k_t, q_t, TN) * SCALE
        top = jnp.max(s, axis=0, keepdims=True)
        e = jnp.exp(s - top)
        total = jnp.sum(e, axis=0, keepdims=True)
        p = (e * (1.0 / total)).astype(BF16)
        lse[0, h:h + 1, :] = top + jnp.log(total)
        mixed[0, lo:lo + HEAD_DIM, :] = dot(v_t, p, NN).astype(BF16)
    middle[...] += dot(mixed[0], w[0, 3 * width:4 * width, :], TN)

    @pl.when(z == nz - 1)
    def _():
        cen, r = row_stats(middle[...])
        n2[...] = (cen * r * g2[...] + b2[...]).astype(BF16)


def ffn_kernel(n, nbuf, idx, *refs):
    gs, refs = refs[:nbuf[0]], refs[nbuf[0]:]
    n2, middle, own_up, own_down, ub, db, g2 = refs[:7]
    refs = refs[7:]
    pa, pb, refs = refs[:nbuf[1]], refs[nbuf[1]:2 * nbuf[1]], refs[2 * nbuf[1]:]
    out, mid_grad, mid_low, keep_u, send_u, keep_d, send_d, dub, sums = refs[:9]
    acc, dn2, n2t, g, up, down, gup, gdown = refs[9:]
    z = pl.program_id(0)
    nz = pl.num_programs(0)
    me = idx[1]
    num = len(gs)

    @pl.when(z == 0)
    def _():
        part_rows = gs[0].shape[0]
        for s, ref in enumerate(gs):
            g[rows_of(lax.rem(idx[2] - s + num, num), part_rows), :] = ref[...]
        acc[...] = middle[...] + db[...]
        dn2[...] = jnp.zeros_like(dn2)
        n2t[...] = n2[...].T
        up[...] = own_up[...]
        down[...] = own_down[...]

    @pl.when(z > 0)
    def _():
        put_pieces(up, 0, pa, me, n, False)
        put_pieces(down, 0, pb, me, n, True)

    u = dot(n2[...], up[...], NN) + ub[0]
    h, slope = gelu_pair(u)
    h = h.astype(BF16)
    acc[...] += dot(h, down[...], NN)
    gdown[...] = dot(h, g[...], TN).astype(BF16)
    pre = (dot(g[...], down[...], NT) * slope).astype(BF16)
    dub[0] = jnp.sum(pre.astype(F32), axis=0, keepdims=True)
    gup[...] = dot(n2t[...], pre, NN).astype(BF16)
    dn2[...] += dot(pre, up[...], NT)
    cut_pieces(gup, 0, keep_u, send_u, me, n, False, gup.shape[0] // n)
    cut_pieces(gdown, 0, keep_d, send_d, me, n, True, gdown.shape[0] // n)

    @pl.when(z == nz - 1)
    def _():
        part_rows = gs[0].shape[0]
        for s in range(num):
            block = rows_of(lax.rem(idx[2] + s, num), part_rows)
            out[s] = acc[block, :].astype(BF16)
        gf = g[...].astype(F32)
        d = dn2[...]
        back, xhat = norm_back(middle[...], d, g2[...])
        mg = gf + back
        mid_grad[...] = mg
        ml = mg.astype(BF16)
        mid_low[...] = ml
        sums[...] = jnp.concatenate([
            jnp.sum(d * xhat, axis=0, keepdims=True),
            jnp.sum(d, axis=0, keepdims=True),
            jnp.sum(ml.astype(F32), axis=0, keepdims=True),
            jnp.sum(gf, axis=0, keepdims=True),
        ], axis=0)


def attn_bwd_kernel(n, nbuf, idx, *refs):
    xs, refs = refs[:nbuf[0]], refs[nbuf[0]:]
    mid_low, mid_grad, start, n1, proj, g1, w, qkv, mixed, lse = refs[:10]
    keep_a, send_a, keep_b, send_b, dqv, tok_grad, sums = refs[10:17]
    dn1, dqkv, gw, xfull, pair, tok = refs[17:]
    z = pl.program_id(0)
    nz = pl.num_programs(0)
    me = idx[1]
    num = len(xs)

    @pl.when(z == 0)
    def _():
        dn1[...] = jnp.zeros_like(dn1)

    ml = mid_low[...]
    width = mixed.shape[1]
    gw[3 * width:4 * width, :] = dot(mixed[0], ml, NN).astype(BF16)
    do_all = dot(w[0, 3 * width:4 * width, :], ml, NT).astype(BF16)
    for h in range(width // HEAD_DIM):
        lo = h * HEAD_DIM
        q_t = qkv[0, lo:lo + HEAD_DIM, :]
        k_t = qkv[0, width + lo:width + lo + HEAD_DIM, :]
        v_t = qkv[0, 2 * width + lo:2 * width + lo + HEAD_DIM, :]
        do_t = do_all[lo:lo + HEAD_DIM, :]
        p = jnp.exp(dot(k_t, q_t, TN) * SCALE - lse[0, h:h + 1, :])
        dp = dot(v_t, do_t, TN)
        dsum = jnp.sum(p * dp, axis=0, keepdims=True)
        ds = (p * (dp - dsum)).astype(BF16)
        dqkv[lo:lo + HEAD_DIM, :] = (dot(k_t, ds, NN) * SCALE).astype(BF16)
        dqkv[width + lo:width + lo + HEAD_DIM, :] = (dot(q_t, ds, NT) * SCALE).astype(BF16)
        dqkv[2 * width + lo:2 * width + lo + HEAD_DIM, :] = dot(do_t, p.astype(BF16), NT).astype(BF16)
    dw = dqkv[...]
    dqv[0] = jnp.sum(dw.astype(F32), axis=1, keepdims=True)
    gw[0:3 * width, :] = dot(dw, n1[...], NN).astype(BF16)
    dn1[...] += dot(dw, w[0, 0:3 * width, :], TN)
    half = 2 * width
    cut_pieces(gw, 0, keep_a, send_a, me, n, False, half // n)
    cut_pieces(gw, half, keep_b, send_b, me, n, True, half // n, at=z)

    @pl.when(z == nz - 1)
    def _():
        part_rows = xs[0].shape[0]
        for s, ref in enumerate(xs):
            xfull[rows_of(lax.rem(idx[2] - s + num, num), part_rows), :] = ref[...]
        d = dn1[...]
        back, xhat = norm_back(start[...], d, g1[...])
        sl = (mid_grad[...] + back).astype(BF16)
        tok[...] = dot(sl, proj[0], NT).astype(BF16)
        for s in range(num):
            tok_grad[s] = tok[rows_of(lax.rem(idx[2] + s, num), part_rows), :]
        feat = proj.shape[1]
        pair[rows_of(idx[0], feat), :] = dot(xfull[...], sl, TN).astype(BF16)
        pair[rows_of(1 - idx[0], feat), :] = jnp.zeros((feat, sl.shape[1]), BF16)
        small = pair.shape[0] // (num * n)
        for i, r in enumerate(kept(n, True)):
            for s in range(num):
                zz = lax.rem(idx[2] - s + num, num)
                for ref, q in ((keep_b, r), (send_b, r | 1)):
                    ref[i, s, half // n:half // n + small, :] = pair[rows_of(zz * n + (me ^ q), small), :]
        sums[...] = jnp.concatenate([
            jnp.sum(sl.astype(F32), axis=0, keepdims=True),
            jnp.sum(d * xhat, axis=0, keepdims=True),
            jnp.sum(d, axis=0, keepdims=True),
            jnp.zeros_like(g1[...]),
        ], axis=0)


def place_kernel(n, sizes, nz, idx, lo, hi, a, b, *c):
    me = idx[1]
    ra, rb = sizes[:2]
    for flip, ref, at, size in ((False, a, 0, ra), (True, b, ra, rb)):
        for i, r in enumerate(kept(n, flip)):
            for src, q in ((lo, r), (hi, r | 1)):
                ref[me ^ q] = src[i, at:at + size, :].astype(F32)
                if c and flip:
                    for s in range(nz):
                        first = ra + rb + s * sizes[2]
                        zz = lax.rem(idx[2] - s + nz, nz)
                        c[0][zz * n + (me ^ q)] = src[i, first:first + sizes[2], :].astype(F32)


def whole(shape):
    return pl.BlockSpec(shape, lambda z, *_: (0,) * len(shape))


def part(shape):
    return pl.BlockSpec((1,) + shape, lambda z, *_: (z,) + (0,) * len(shape))


def true_part(shape, nz):
    return pl.BlockSpec((1,) + shape, lambda z, k: (lax.rem(k[2] - z + nz, nz),) + (0,) * len(shape))


def by_kind(shape):
    return pl.BlockSpec((1,) + shape, lambda z, k: (k[0],) + (0,) * len(shape))


def piece_in(v):
    k, _, r, d = v.shape
    return pl.BlockSpec((k, 1, r, d), lambda z, *_: (0, jnp.maximum(z - 1, 0), 0, 0))


def piece_out(k, r, d):
    return pl.BlockSpec((k, 1, r, d), lambda z, *_: (0, z, 0, 0))


def sds(shape, dtype):
    return jax.ShapeDtypeStruct(shape, dtype)


PARAMS = pltpu.CompilerParams(dimension_semantics=("arbitrary",), vmem_limit_bytes=58 << 20)


def call(kernel, grid, args, in_specs, outs, scratch, name):
    return pl.pallas_call(
        kernel,
        grid_spec=pltpu.PrefetchScalarGridSpec(
            num_scalar_prefetch=1, grid=grid, in_specs=in_specs, out_specs=[s for s, _ in outs],
            scratch_shapes=scratch),
        out_shape=[o for _, o in outs], compiler_params=PARAMS, name=name,
    )(*args)


def attn_fwd(n, nz, idx, xs, proj, pbias, g1, b1, own_a, own_b, bq, ob, g2, b2, pa, pb):
    rows, feat = xs[0].shape
    half, d = own_a.shape
    hw = half // 2
    seq = rows * nz
    row = (1, d)
    return call(
        functools.partial(attn_fwd_kernel, n, (nz, len(pa))), (nz,),
        (idx, *xs, proj, pbias, g1, b1, own_a, own_b, bq, ob, g2, b2, *pa, *pb),
        [whole((rows, feat))] * nz + [by_kind((feat, d)), by_kind(row), whole(row), whole(row),
                                      whole((half, d)), whole((half, d)), part((3 * hw, 1)),
                                      whole(row), whole(row), whole(row)]
        + [piece_in(v) for v in (*pa, *pb)],
        [(whole((seq, d)), sds((seq, d), F32)), (whole((seq, d)), sds((seq, d), BF16)),
         (part((3 * hw, seq)), sds((nz, 3 * hw, seq), BF16)), (part((hw, seq)), sds((nz, hw, seq), BF16)),
         (part((8, seq)), sds((nz, 8, seq), F32)), (whole((seq, d)), sds((seq, d), F32)),
         (whole((seq, d)), sds((seq, d), BF16)), (part((2 * half, d)), sds((nz, 2 * half, d), BF16))],
        [pltpu.VMEM((seq, feat), BF16)], "attn_fwd")


def ffn(n, nz, idx, gs, n2, middle, own_up, own_down, ub, db, g2, pa, pb):
    rows, d = gs[0].shape
    f = own_up.shape[1]
    seq = rows * nz
    row = (1, d)
    h = n // 2
    return call(
        functools.partial(ffn_kernel, n, (nz, len(pa))), (nz,),
        (idx, *gs, n2, middle, own_up, own_down, ub, db, g2, *pa, *pb),
        [whole((rows, d))] * nz + [whole((seq, d)), whole((seq, d)), whole((d, f)), whole((f, d)),
                                   true_part((1, f), nz), whole(row), whole(row)]
        + [piece_in(v) for v in (*pa, *pb)],
        [(whole((nz, rows, d)), sds((nz, rows, d), BF16)), (whole((seq, d)), sds((seq, d), F32)),
         (whole((seq, d)), sds((seq, d), BF16)),
         (piece_out(h, d // n, f), sds((h, nz, d // n, f), BF16)),
         (piece_out(h, d // n, f), sds((h, nz, d // n, f), BF16)),
         (piece_out(h, f // n, d), sds((h, nz, f // n, d), BF16)),
         (piece_out(h, f // n, d), sds((h, nz, f // n, d), BF16)),
         (true_part((1, f), nz), sds((nz, 1, f), F32)), (whole((4, d)), sds((4, d), F32))],
        [pltpu.VMEM((seq, d), F32), pltpu.VMEM((seq, d), F32), pltpu.VMEM((d, seq), BF16),
         pltpu.VMEM((seq, d), BF16), pltpu.VMEM((d, f), BF16), pltpu.VMEM((f, d), BF16),
         pltpu.VMEM((d, f), BF16), pltpu.VMEM((f, d), BF16)], "ffn")


def attn_bwd(n, nz, idx, xs, mid_low, mid_grad, start, n1, proj, g1, w, qkv, mixed, lse):
    rows, feat = xs[0].shape
    seq, d = n1.shape
    hw = mixed.shape[1]
    row = (1, d)
    h = n // 2
    ra = 2 * hw // n
    rb = ra + proj.shape[0] * feat // (nz * n)
    return call(
        functools.partial(attn_bwd_kernel, n, (nz,)), (nz,),
        (idx, *xs, mid_low, mid_grad, start, n1, proj, g1, w, qkv, mixed, lse),
        [whole((rows, feat))] * nz + [whole((seq, d)), whole((seq, d)), whole((seq, d)), whole((seq, d)),
                                      by_kind((feat, d)), whole(row), part((4 * hw, d)),
                                      part((3 * hw, seq)), part((hw, seq)), part((8, seq))],
        [(piece_out(h, ra, d), sds((h, nz, ra, d), BF16)), (piece_out(h, ra, d), sds((h, nz, ra, d), BF16)),
         (whole((h, nz, rb, d)), sds((h, nz, rb, d), BF16)), (whole((h, nz, rb, d)), sds((h, nz, rb, d), BF16)),
         (true_part((3 * hw, 1), nz), sds((nz, 3 * hw, 1), F32)),
         (whole((nz, rows, feat)), sds((nz, rows, feat), BF16)), (whole((4, d)), sds((4, d), F32))],
        [pltpu.VMEM((seq, d), F32), pltpu.VMEM((3 * hw, seq), BF16), pltpu.VMEM((4 * hw, d), BF16),
         pltpu.VMEM((seq, feat), BF16), pltpu.VMEM((proj.shape[0] * feat, d), BF16),
         pltpu.VMEM((seq, feat), BF16)], "attn_bwd")


def place(n, nz, idx, lo, hi, sizes):
    h, rows, d = lo.shape
    col = 256 if d % 256 == 0 else d
    outs = [(n, sizes[0]), (n, sizes[1])] + [(n * nz, s) for s in sizes[2:]]
    spec = lambda a, b: pl.BlockSpec((a, b, col), lambda j, *_: (0, 0, j))
    return call(
        functools.partial(place_kernel, n, sizes, nz), (d // col,), (idx, lo, hi), [spec(h, rows)] * 2,
        [(spec(a, b), sds((a, b, d), F32)) for a, b in outs], [], "place")


def per_device(nw, nz, tokens, kind, proj_weight, proj_bias, ln1_gain, ln1_bias, qkv_weight, qv_bias,
               out_weight, out_bias, ln2_gain, ln2_bias, up_weight, up_bias, down_weight, down_bias,
               cotangent):
    d, f = up_weight.shape
    hw = out_weight.shape[0]
    feat = tokens.shape[2]
    n = min(nw, 8)
    me_w = lax.axis_index("wide")
    me_z = lax.axis_index("narrow")
    me = lax.rem(me_w, n)
    my_kind = lax.dynamic_index_in_dim(kind, me_z, 0, keepdims=False)
    idx = jnp.stack([jnp.where(my_kind == 1, 1, 0), me, me_z]).astype(jnp.int32)

    def swap(v, bit):
        return lax.ppermute(v, "wide", [(i, i ^ bit) for i in range(nw)])

    def shift(v, s):
        return lax.ppermute(v, "narrow", [(i, (i + s) % nz) for i in range(nz)])

    def add(a, b):
        return (a.astype(F32) + b.astype(F32)).astype(BF16)

    def to_clip(v):
        return [lax.dynamic_index_in_dim(v, me_z, 0, keepdims=False)] + [
            shift(lax.dynamic_index_in_dim(v, lax.rem(me_z + s, nz), 0, keepdims=False), s)
            for s in range(1, nz)]

    def to_rows(v):
        got = [v[0]] + [shift(v[s], s) for s in range(1, nz)]
        ring = jnp.stack([got[-k % nz] for k in range(nz)] * 2)
        return lax.dynamic_slice_in_dim(ring, nz - me_z, nz, 0)

    def spread(cur, flip, last):
        bufs = [cur]
        for b in step_bits(n, flip)[::-1]:
            now = jnp.concatenate(bufs) if len(bufs) > 1 else bufs[0]
            bufs = [now, swap(now, b)]
        return bufs + [swap(v, 1) for v in bufs] if last else jnp.concatenate(bufs)

    def gather(a, b):
        ra, rb = a.shape[0] // n, b.shape[0] // n
        mine = jnp.concatenate([lax.dynamic_slice_in_dim(a, me * ra, ra, 0),
                                lax.dynamic_slice_in_dim(b, me * rb, rb, 0)])
        got = jnp.stack([shift(mine, s) for s in range(1, nz)])
        return spread(got[None, :, :ra], False, True), spread(got[None, :, ra:], True, True)

    def fold(keep, send, flip):
        got = swap(send, 1)
        for b in step_bits(n, flip):
            h = keep.shape[0] // 2
            go = add(keep[h:], got[h:])
            keep, got = add(keep[:h], got[:h]), swap(go, b)
        total = add(keep[0], got[0])
        for k in range(n.bit_length() - 1, nw.bit_length() - 1):
            total = add(total, swap(total, 1 << k))
        return total

    def over_z(a, b):
        ra = a.shape[1]
        total = [a[0].astype(F32), b[0].astype(F32)]
        for s in range(1, nz):
            got = shift(jnp.concatenate([a[s], b[s]]), -s)
            total = [total[0] + got[:ra].astype(F32), total[1] + got[ra:].astype(F32)]
        return total[0].astype(BF16), total[1].astype(BF16)

    def share(a, b, sizes):
        lo = jnp.concatenate([spread(a[None], False, False), spread(b[None], True, False)], axis=1)
        return place(n, nz, idx, lo, swap(lo, 1), sizes)

    xs = to_clip(tokens)
    bias_three = jnp.concatenate([qv_bias[0], jnp.zeros_like(qv_bias[0]), qv_bias[1]])
    bq = jnp.stack([bias_three] + [shift(bias_three, s) for s in range(1, nz)])[:, :, None]
    qkv_t = jnp.transpose(qkv_weight, (1, 2, 0))
    own_a = qkv_t[:2].reshape(2 * hw, d)
    own_b = jnp.concatenate([qkv_t[2], out_weight])
    pa, pb = gather(own_a, own_b)
    fa, fb = gather(up_weight, down_weight)
    gs = to_clip(cotangent)
    r = lambda v: v.reshape(1, d)

    start, n1, qkv, mixed, lse, middle, n2, w = attn_fwd(
        n, nz, idx, xs, proj_weight, proj_bias[:, None, :], r(ln1_gain), r(ln1_bias), own_a, own_b, bq,
        r(out_bias), r(ln2_gain), r(ln2_bias), pa, pb)
    out, mid_grad, mid_low, keep_u, send_u, keep_d, send_d, dub, sums2 = ffn(
        n, nz, idx, gs, n2, middle, up_weight, down_weight, up_bias.reshape(nz, 1, f), r(down_bias),
        r(ln2_gain), fa, fb)
    keep_a, send_a, keep_b, send_b, dqv, tok_grad, sums1 = attn_bwd(
        n, nz, idx, xs, mid_low, mid_grad, start, n1, proj_weight, r(ln1_gain), w, qkv, mixed, lse)

    up_z, down_z = over_z(fold(keep_u, send_u, False), fold(keep_d, send_d, True))
    output = to_rows(out)
    up_g, down_g = share(up_z, down_z, (d // n, f // n))

    tokens_grad = to_rows(tok_grad).astype(F32)
    a_z, b_z = over_z(fold(keep_a, send_a, False), fold(keep_b, send_b, True))
    ra = 2 * hw // n
    tail = b_z[ra:]
    b_all = jnp.concatenate([b_z[:ra], tail] + [shift(tail, s) for s in range(1, nz)])
    a_g, b_g, proj_g = share(a_z, b_all, (ra, ra, tail.shape[0]))

    is_patch = idx[0] == 1
    bias_pair = jnp.stack([jnp.where(is_patch, 0.0, sums1[0]), jnp.where(is_patch, sums1[0], 0.0)])
    dqv_cols = dqv.reshape(nz, 3, hw)
    small = jnp.concatenate([
        bias_pair, sums1[1:3], sums2, dub.reshape(nz, f).reshape(-1, d),
        dqv_cols[:, 0].reshape(-1, d), dqv_cols[:, 2].reshape(-1, d)], axis=0)
    for k in range(nw.bit_length() - 1):
        small = small + swap(small, 1 << k)
    for k in range(nz.bit_length() - 1):
        small = small + lax.ppermute(small, "narrow", [(i, i ^ (1 << k)) for i in range(nz)])
    last = 8 + nz * f // d
    up_b = lax.dynamic_index_in_dim(small[8:last].reshape(nz, f), me_z, 0, keepdims=False)
    qv = lax.dynamic_slice_in_dim(small[last:].reshape(2, nz * hw), me_z * hw, hw, 1)
    a_g = a_g.reshape(2 * hw, d)
    b_g = b_g.reshape(2 * hw, d)
    qkv_g = jnp.transpose(jnp.concatenate([a_g, b_g[:hw]]).reshape(3, hw, d), (2, 0, 1))
    return (output, tokens_grad, proj_g.reshape(-1, feat, d), small[0:2], small[2], small[3], qkv_g, qv,
            b_g[hw:], small[6], small[4], small[5], up_g.reshape(d, f), up_b, down_g.reshape(f, d),
            small[7])


def solution(mesh):
    in_specs = (
        P("wide", "narrow", None), P("wide"), P(), P(), P(), P(), P(None, None, "narrow"),
        P(None, "narrow"), P("narrow", None), P(), P(), P(), P(None, "narrow"), P(),
        P("narrow", None), P(), P("wide", "narrow", None),
    )
    out_specs = (
        P("wide", "narrow", None), P("wide", "narrow", None), P(), P(), P(), P(),
        P(None, None, "narrow"), P(None, "narrow"), P("narrow", None), P(), P(), P(),
        P(None, "narrow"), P("narrow"), P("narrow", None), P(),
    )
    body = functools.partial(per_device, mesh.shape["wide"], mesh.shape["narrow"])
    return jax.shard_map(
        body, mesh=mesh, in_specs=in_specs, out_specs=out_specs, check_vma=False
    )
```

```python
import functools

import jax
import jax.numpy as jnp
from jax import lax
from jax.experimental import pallas as pl
from jax.experimental.pallas import tpu as pltpu
from jax.sharding import PartitionSpec as P


HEAD_DIM = 64
SCALE = HEAD_DIM ** (-0.5)
EPS = 1e-06
F32 = jnp.float32
BF16 = jnp.bfloat16
NN = (((1,), (0,)), ((), ()))
NT = (((1,), (1,)), ((), ()))
TN = (((0,), (0,)), ((), ()))


def dot(a, b, dims):
    return lax.dot_general(a, b, dims, preferred_element_type=F32)


def row_stats(v):
    mean = jnp.mean(v, axis=-1, keepdims=True)
    cen = v - mean
    var = jnp.mean(cen * cen, axis=-1, keepdims=True)
    return cen, lax.rsqrt(var + EPS)


def norm_back(v, grad, gain):
    cen, r = row_stats(v)
    xhat = cen * r
    q = grad * gain
    mq = jnp.mean(q, axis=-1, keepdims=True)
    mqx = jnp.mean(q * xhat, axis=-1, keepdims=True)
    return r * (q - mq - xhat * mqx), xhat


def gelu_pair(u):
    phi = 0.5 * (1.0 + lax.erf(u * (2.0 ** -0.5)))
    dens = jnp.exp(-0.5 * u * u) * 0.3989422804014327
    return u * phi, phi + u * dens


def rows_of(i, size):
    start = i * size
    return pl.ds(pl.multiple_of(start, size & -size), size)


def step_bits(n, flip):
    bits = [1 << k for k in range(1, n.bit_length() - 1)]
    return bits[::-1] if flip else bits


def kept(n, flip):
    order = [0]
    for b in step_bits(n, flip)[::-1]:
        order = order + [r | b for r in order]
    return order


def spread_order(n, flip):
    bits = step_bits(n, flip)[::-1]
    sets = [[0]]
    for b in bits:
        now = [r for one in sets for r in one]
        sets = [now, [r ^ b for r in now]]
    return sets + [[r ^ 1 for r in one] for one in sets]


def put_pieces(dst, base, bufs, me, n, flip):
    for ref, rs in zip(bufs, spread_order(n, flip)):
        size = ref.shape[2]
        for i, r in enumerate(rs):
            dst[rows_of(base // size + (me ^ r), size), :] = ref[i, 0]


def cut_pieces(src, base, keep, send, me, n, flip, size, at=None):
    for i, r in enumerate(kept(n, flip)):
        for ref, q in ((keep, r), (send, r | 1)):
            val = src[rows_of(base // size + (me ^ q), size), :]
            if at is None:
                ref[i, 0] = val
            else:
                ref[i, at, 0:size] = val


def attn_fwd_kernel(n, nbuf, idx, *refs):
    xs, refs = refs[:nbuf[0]], refs[nbuf[0]:]
    proj, pbias, g1, b1, own_a, own_b, bq, ob, g2, b2 = refs[:10]
    refs = refs[10:]
    pa, pb, refs = refs[:nbuf[1]], refs[nbuf[1]:2 * nbuf[1]], refs[2 * nbuf[1]:]
    start, n1, qkv, mixed, lse, middle, n2, w, xfull = refs
    z = pl.program_id(0)
    nz = pl.num_programs(0)
    me = idx[1]
    half = own_a.shape[0]

    @pl.when(z == 0)
    def _():
        part_rows = xs[0].shape[0]
        for s, ref in enumerate(xs):
            xfull[rows_of(lax.rem(idx[2] - s + len(xs), len(xs)), part_rows), :] = ref[...]
        s = dot(xfull[...], proj[0], NN) + pbias[0]
        start[...] = s
        middle[...] = s + ob[...]
        cen, r = row_stats(s)
        n1[...] = (cen * r * g1[...] + b1[...]).astype(BF16)
        w[0, 0:half, :] = own_a[...]
        w[0, half:2 * half, :] = own_b[...]

    @pl.when(z > 0)
    def _():
        put_pieces(w.at[0], 0, pa, me, n, False)
        put_pieces(w.at[0], half, pb, me, n, True)

    width = mixed.shape[1]
    qkv[0] = (dot(w[0, 0:3 * width, :], n1[...], NT) + bq[0]).astype(BF16)
    for h in range(width // HEAD_DIM):
        lo = h * HEAD_DIM
        q_t = qkv[0, lo:lo + HEAD_DIM, :]
        k_t = qkv[0, width + lo:width + lo + HEAD_DIM, :]
        v_t = qkv[0, 2 * width + lo:2 * width + lo + HEAD_DIM, :]
        s = dot(k_t, q_t, TN) * SCALE
        top = jnp.max(s, axis=0, keepdims=True)
        e = jnp.exp(s - top)
        total = jnp.sum(e, axis=0, keepdims=True)
        p = (e * (1.0 / total)).astype(BF16)
        lse[0, h:h + 1, :] = top + jnp.log(total)
        mixed[0, lo:lo + HEAD_DIM, :] = dot(v_t, p, NN).astype(BF16)
    middle[...] += dot(mixed[0], w[0, 3 * width:4 * width, :], TN)

    @pl.when(z == nz - 1)
    def _():
        cen, r = row_stats(middle[...])
        n2[...] = (cen * r * g2[...] + b2[...]).astype(BF16)


def ffn_kernel(n, nbuf, idx, *refs):
    gs, refs = refs[:nbuf[0]], refs[nbuf[0]:]
    n2, middle, own_up, own_down, ub, db, g2 = refs[:7]
    refs = refs[7:]
    pa, pb, refs = refs[:nbuf[1]], refs[nbuf[1]:2 * nbuf[1]], refs[2 * nbuf[1]:]
    out, mid_grad, mid_low, keep_u, send_u, keep_d, send_d, dub, sums = refs[:9]
    acc, dn2, n2t, g, up, down, gup, gdown = refs[9:]
    z = pl.program_id(0)
    nz = pl.num_programs(0)
    me = idx[1]
    num = len(gs)

    @pl.when(z == 0)
    def _():
        part_rows = gs[0].shape[0]
        for s, ref in enumerate(gs):
            g[rows_of(lax.rem(idx[2] - s + num, num), part_rows), :] = ref[...]
        acc[...] = middle[...] + db[...]
        dn2[...] = jnp.zeros_like(dn2)
        n2t[...] = n2[...].T
        up[...] = own_up[...]
        down[...] = own_down[...]

    @pl.when(z > 0)
    def _():
        put_pieces(up, 0, pa, me, n, False)
        put_pieces(down, 0, pb, me, n, True)

    u = dot(n2[...], up[...], NN) + ub[0]
    h, slope = gelu_pair(u)
    h = h.astype(BF16)
    acc[...] += dot(h, down[...], NN)
    gdown[...] = dot(h, g[...], TN).astype(BF16)
    pre = (dot(g[...], down[...], NT) * slope).astype(BF16)
    dub[0] = jnp.sum(pre.astype(F32), axis=0, keepdims=True)
    gup[...] = dot(n2t[...], pre, NN).astype(BF16)
    dn2[...] += dot(pre, up[...], NT)
    cut_pieces(gup, 0, keep_u, send_u, me, n, False, gup.shape[0] // n)
    cut_pieces(gdown, 0, keep_d, send_d, me, n, True, gdown.shape[0] // n)

    @pl.when(z == nz - 1)
    def _():
        part_rows = gs[0].shape[0]
        for s in range(num):
            block = rows_of(lax.rem(idx[2] + s, num), part_rows)
            out[s] = acc[block, :].astype(BF16)
        gf = g[...].astype(F32)
        d = dn2[...]
        back, xhat = norm_back(middle[...], d, g2[...])
        mg = gf + back
        mid_grad[...] = mg
        ml = mg.astype(BF16)
        mid_low[...] = ml
        sums[...] = jnp.concatenate([
            jnp.sum(d * xhat, axis=0, keepdims=True),
            jnp.sum(d, axis=0, keepdims=True),
            jnp.sum(ml.astype(F32), axis=0, keepdims=True),
            jnp.sum(gf, axis=0, keepdims=True),
        ], axis=0)


def attn_bwd_kernel(n, nbuf, idx, *refs):
    xs, refs = refs[:nbuf[0]], refs[nbuf[0]:]
    mid_low, mid_grad, start, n1, proj, g1, w, qkv, mixed, lse = refs[:10]
    keep_a, send_a, keep_b, send_b, dqv, tok_grad, sums = refs[10:17]
    dn1, dqkv, gw, xfull, pair, tok = refs[17:]
    z = pl.program_id(0)
    nz = pl.num_programs(0)
    me = idx[1]
    num = len(xs)

    @pl.when(z == 0)
    def _():
        dn1[...] = jnp.zeros_like(dn1)

    ml = mid_low[...]
    width = mixed.shape[1]
    gw[3 * width:4 * width, :] = dot(mixed[0], ml, NN).astype(BF16)
    do_all = dot(w[0, 3 * width:4 * width, :], ml, NT).astype(BF16)
    for h in range(width // HEAD_DIM):
        lo = h * HEAD_DIM
        q_t = qkv[0, lo:lo + HEAD_DIM, :]
        k_t = qkv[0, width + lo:width + lo + HEAD_DIM, :]
        v_t = qkv[0, 2 * width + lo:2 * width + lo + HEAD_DIM, :]
        do_t = do_all[lo:lo + HEAD_DIM, :]
        p = jnp.exp(dot(k_t, q_t, TN) * SCALE - lse[0, h:h + 1, :])
        dp = dot(v_t, do_t, TN)
        dsum = jnp.sum(p * dp, axis=0, keepdims=True)
        ds = (p * (dp - dsum)).astype(BF16)
        dqkv[lo:lo + HEAD_DIM, :] = (dot(k_t, ds, NN) * SCALE).astype(BF16)
        dqkv[width + lo:width + lo + HEAD_DIM, :] = (dot(q_t, ds, NT) * SCALE).astype(BF16)
        dqkv[2 * width + lo:2 * width + lo + HEAD_DIM, :] = dot(do_t, p.astype(BF16), NT).astype(BF16)
    dw = dqkv[...]
    dqv[0] = jnp.sum(dw.astype(F32), axis=1, keepdims=True)
    gw[0:3 * width, :] = dot(dw, n1[...], NN).astype(BF16)
    dn1[...] += dot(dw, w[0, 0:3 * width, :], TN)
    half = 2 * width
    cut_pieces(gw, 0, keep_a, send_a, me, n, False, half // n)
    cut_pieces(gw, half, keep_b, send_b, me, n, True, half // n, at=z)

    @pl.when(z == nz - 1)
    def _():
        part_rows = xs[0].shape[0]
        for s, ref in enumerate(xs):
            xfull[rows_of(lax.rem(idx[2] - s + num, num), part_rows), :] = ref[...]
        d = dn1[...]
        back, xhat = norm_back(start[...], d, g1[...])
        sl = (mid_grad[...] + back).astype(BF16)
        tok[...] = dot(sl, proj[0], NT).astype(BF16)
        for s in range(num):
            tok_grad[s] = tok[rows_of(lax.rem(idx[2] + s, num), part_rows), :]
        feat = proj.shape[1]
        pair[rows_of(idx[0], feat), :] = dot(xfull[...], sl, TN).astype(BF16)
        pair[rows_of(1 - idx[0], feat), :] = jnp.zeros((feat, sl.shape[1]), BF16)
        small = pair.shape[0] // (num * n)
        for i, r in enumerate(kept(n, True)):
            for s in range(num):
                zz = lax.rem(idx[2] - s + num, num)
                for ref, q in ((keep_b, r), (send_b, r | 1)):
                    ref[i, s, half // n:half // n + small, :] = pair[rows_of(zz * n + (me ^ q), small), :]
        sums[...] = jnp.concatenate([
            jnp.sum(sl.astype(F32), axis=0, keepdims=True),
            jnp.sum(d * xhat, axis=0, keepdims=True),
            jnp.sum(d, axis=0, keepdims=True),
            jnp.zeros_like(g1[...]),
        ], axis=0)


def place_kernel(n, sizes, nz, idx, lo, hi, a, b, *c):
    me = idx[1]
    ra, rb = sizes[:2]
    for flip, ref, at, size in ((False, a, 0, ra), (True, b, ra, rb)):
        for i, r in enumerate(kept(n, flip)):
            for src, q in ((lo, r), (hi, r | 1)):
                ref[me ^ q] = src[i, at:at + size, :].astype(F32)
                if c and flip:
                    for s in range(nz):
                        first = ra + rb + s * sizes[2]
                        zz = lax.rem(idx[2] - s + nz, nz)
                        c[0][zz * n + (me ^ q)] = src[i, first:first + sizes[2], :].astype(F32)


def whole(shape):
    return pl.BlockSpec(shape, lambda z, *_: (0,) * len(shape))


def part(shape):
    return pl.BlockSpec((1,) + shape, lambda z, *_: (z,) + (0,) * len(shape))


def true_part(shape, nz):
    return pl.BlockSpec((1,) + shape, lambda z, k: (lax.rem(k[2] - z + nz, nz),) + (0,) * len(shape))


def by_kind(shape):
    return pl.BlockSpec((1,) + shape, lambda z, k: (k[0],) + (0,) * len(shape))


def piece_in(v):
    k, _, r, d = v.shape
    return pl.BlockSpec((k, 1, r, d), lambda z, *_: (0, jnp.maximum(z - 1, 0), 0, 0))


def piece_out(k, r, d):
    return pl.BlockSpec((k, 1, r, d), lambda z, *_: (0, z, 0, 0))


def sds(shape, dtype):
    return jax.ShapeDtypeStruct(shape, dtype)


PARAMS = pltpu.CompilerParams(dimension_semantics=("arbitrary",), vmem_limit_bytes=58 << 20)


def work(us):
    return us * 10 ** 9, us * 10 ** 6, 0


def call(kernel, grid, args, in_specs, outs, scratch, cost=(0, 0, 0)):
    estimate = pl.CostEstimate(flops=cost[0], bytes_accessed=cost[1], transcendentals=cost[2])
    return pl.pallas_call(
        kernel,
        grid_spec=pltpu.PrefetchScalarGridSpec(
            num_scalar_prefetch=1, grid=grid, in_specs=in_specs, out_specs=[s for s, _ in outs],
            scratch_shapes=scratch),
        out_shape=[o for _, o in outs], compiler_params=PARAMS, cost_estimate=estimate,
    )(*args)


def attn_fwd(n, nz, idx, xs, proj, pbias, g1, b1, own_a, own_b, bq, ob, g2, b2, pa, pb):
    rows, feat = xs[0].shape
    half, d = own_a.shape
    hw = half // 2
    seq = rows * nz
    row = (1, d)
    return call(
        functools.partial(attn_fwd_kernel, n, (nz, len(pa))), (nz,),
        (idx, *xs, proj, pbias, g1, b1, own_a, own_b, bq, ob, g2, b2, *pa, *pb),
        [whole((rows, feat))] * nz + [by_kind((feat, d)), by_kind(row), whole(row), whole(row),
                                      whole((half, d)), whole((half, d)), part((3 * hw, 1)),
                                      whole(row), whole(row), whole(row)]
        + [piece_in(v) for v in (*pa, *pb)],
        [(whole((seq, d)), sds((seq, d), F32)), (whole((seq, d)), sds((seq, d), BF16)),
         (part((3 * hw, seq)), sds((nz, 3 * hw, seq), BF16)), (part((hw, seq)), sds((nz, hw, seq), BF16)),
         (part((8, seq)), sds((nz, 8, seq), F32)), (whole((seq, d)), sds((seq, d), F32)),
         (whole((seq, d)), sds((seq, d), BF16)), (part((2 * half, d)), sds((nz, 2 * half, d), BF16))],
        [pltpu.VMEM((seq, feat), BF16)], work(20))


def ffn(n, nz, idx, gs, n2, middle, own_up, own_down, ub, db, g2, pa, pb):
    rows, d = gs[0].shape
    f = own_up.shape[1]
    seq = rows * nz
    row = (1, d)
    h = n // 2
    return call(
        functools.partial(ffn_kernel, n, (nz, len(pa))), (nz,),
        (idx, *gs, n2, middle, own_up, own_down, ub, db, g2, *pa, *pb),
        [whole((rows, d))] * nz + [whole((seq, d)), whole((seq, d)), whole((d, f)), whole((f, d)),
                                   true_part((1, f), nz), whole(row), whole(row)]
        + [piece_in(v) for v in (*pa, *pb)],
        [(whole((nz, rows, d)), sds((nz, rows, d), BF16)), (whole((seq, d)), sds((seq, d), F32)),
         (whole((seq, d)), sds((seq, d), BF16)),
         (piece_out(h, d // n, f), sds((h, nz, d // n, f), BF16)),
         (piece_out(h, d // n, f), sds((h, nz, d // n, f), BF16)),
         (piece_out(h, f // n, d), sds((h, nz, f // n, d), BF16)),
         (piece_out(h, f // n, d), sds((h, nz, f // n, d), BF16)),
         (true_part((1, f), nz), sds((nz, 1, f), F32)), (whole((4, d)), sds((4, d), F32))],
        [pltpu.VMEM((seq, d), F32), pltpu.VMEM((seq, d), F32), pltpu.VMEM((d, seq), BF16),
         pltpu.VMEM((seq, d), BF16), pltpu.VMEM((d, f), BF16), pltpu.VMEM((f, d), BF16),
         pltpu.VMEM((d, f), BF16), pltpu.VMEM((f, d), BF16)], work(26))


def attn_bwd(n, nz, idx, xs, mid_low, mid_grad, start, n1, proj, g1, w, qkv, mixed, lse):
    rows, feat = xs[0].shape
    seq, d = n1.shape
    hw = mixed.shape[1]
    row = (1, d)
    h = n // 2
    ra = 2 * hw // n
    rb = ra + proj.shape[0] * feat // (nz * n)
    return call(
        functools.partial(attn_bwd_kernel, n, (nz,)), (nz,),
        (idx, *xs, mid_low, mid_grad, start, n1, proj, g1, w, qkv, mixed, lse),
        [whole((rows, feat))] * nz + [whole((seq, d)), whole((seq, d)), whole((seq, d)), whole((seq, d)),
                                      by_kind((feat, d)), whole(row), part((4 * hw, d)),
                                      part((3 * hw, seq)), part((hw, seq)), part((8, seq))],
        [(piece_out(h, ra, d), sds((h, nz, ra, d), BF16)), (piece_out(h, ra, d), sds((h, nz, ra, d), BF16)),
         (whole((h, nz, rb, d)), sds((h, nz, rb, d), BF16)), (whole((h, nz, rb, d)), sds((h, nz, rb, d), BF16)),
         (true_part((3 * hw, 1), nz), sds((nz, 3 * hw, 1), F32)),
         (whole((nz, rows, feat)), sds((nz, rows, feat), BF16)), (whole((4, d)), sds((4, d), F32))],
        [pltpu.VMEM((seq, d), F32), pltpu.VMEM((3 * hw, seq), BF16), pltpu.VMEM((4 * hw, d), BF16),
         pltpu.VMEM((seq, feat), BF16), pltpu.VMEM((proj.shape[0] * feat, d), BF16),
         pltpu.VMEM((seq, feat), BF16)], work(26))


def place(n, nz, idx, lo, hi, sizes):
    h, rows, d = lo.shape
    col = 256 if d % 256 == 0 else d
    outs = [(n, sizes[0]), (n, sizes[1])] + [(n * nz, s) for s in sizes[2:]]
    spec = lambda a, b: pl.BlockSpec((a, b, col), lambda j, *_: (0, 0, j))
    return call(
        functools.partial(place_kernel, n, sizes, nz), (d // col,), (idx, lo, hi), [spec(h, rows)] * 2,
        [(spec(a, b), sds((a, b, d), F32)) for a, b in outs], [], work(5))


def line_up_kernel(idx, *refs):
    num = len(refs) - 1
    for s, ref in enumerate(refs[:num]):
        refs[num][lax.rem(idx[2] - s + num, num)] = ref[...].astype(refs[num].dtype)


def line_up(nz, idx, blocks, dtype):
    rows, d = blocks[0].shape
    return call(
        line_up_kernel, (1,), (idx, *blocks), [whole((rows, d))] * nz,
        [(whole((nz, rows, d)), sds((nz, rows, d), dtype))], [], work(2))[0]


def per_device(nw, nz, tokens, kind, proj_weight, proj_bias, ln1_gain, ln1_bias, qkv_weight, qv_bias,
               out_weight, out_bias, ln2_gain, ln2_bias, up_weight, up_bias, down_weight, down_bias,
               cotangent):
    d, f = up_weight.shape
    hw = out_weight.shape[0]
    feat = tokens.shape[2]
    n = min(nw, 8)
    me_w = lax.axis_index("wide")
    me_z = lax.axis_index("narrow")
    me = lax.rem(me_w, n)
    my_kind = lax.dynamic_index_in_dim(kind, me_z, 0, keepdims=False)
    idx = jnp.stack([jnp.where(my_kind == 1, 1, 0), me, me_z]).astype(jnp.int32)

    def swap(v, bit):
        return lax.ppermute(v, "wide", [(i, i ^ bit) for i in range(nw)])

    def shift(v, s):
        return lax.ppermute(v, "narrow", [(i, (i + s) % nz) for i in range(nz)])

    def add(a, b):
        return (a.astype(F32) + b.astype(F32)).astype(BF16)

    def to_clip(v):
        return [lax.dynamic_index_in_dim(v, me_z, 0, keepdims=False)] + [
            shift(lax.dynamic_index_in_dim(v, lax.rem(me_z + s, nz), 0, keepdims=False), s)
            for s in range(1, nz)]

    def to_rows(v, dtype):
        return line_up(nz, idx, [v[0]] + [shift(v[s], s) for s in range(1, nz)], dtype)

    def spread(cur, flip, last):
        bufs = [cur]
        for b in step_bits(n, flip)[::-1]:
            now = jnp.concatenate(bufs) if len(bufs) > 1 else bufs[0]
            bufs = [now, swap(now, b)]
        if not last:
            return jnp.concatenate(bufs)
        return bufs + [swap(v, 1) for v in bufs]

    def gather(a, b):
        ra, rb = a.shape[0] // n, b.shape[0] // n
        mine = jnp.concatenate([lax.dynamic_slice_in_dim(a, me * ra, ra, 0),
                                lax.dynamic_slice_in_dim(b, me * rb, rb, 0)])
        got = jnp.stack([shift(mine, s) for s in range(1, nz)])
        return (spread(got[None, :, :ra], False, True),
                spread(got[None, :, ra:], True, True))

    def fold(keep, send, flip):
        got = swap(send, 1)
        for b in step_bits(n, flip):
            h = keep.shape[0] // 2
            go = add(keep[h:], got[h:])
            keep, got = add(keep[:h], got[:h]), swap(go, b)
        total = add(keep[0], got[0])
        for k in range(n.bit_length() - 1, nw.bit_length() - 1):
            total = add(total, swap(total, 1 << k))
        return total

    def over_z(a, b):
        ra = a.shape[1]
        total = [a[0].astype(F32), b[0].astype(F32)]
        for s in range(1, nz):
            both = jnp.concatenate([a[s], b[s]])
            got = shift(both, -s)
            total = [total[0] + got[:ra].astype(F32), total[1] + got[ra:].astype(F32)]
        return total[0].astype(BF16), total[1].astype(BF16)

    def share(a, b, sizes):
        lo = jnp.concatenate([spread(a[None], False, False),
                              spread(b[None], True, False)], axis=1)
        return place(n, nz, idx, lo, swap(lo, 1), sizes)

    xs = to_clip(tokens)
    bias_three = jnp.concatenate([qv_bias[0], jnp.zeros_like(qv_bias[0]), qv_bias[1]])
    bq = jnp.stack([bias_three] + [shift(bias_three, s) for s in range(1, nz)])[:, :, None]
    qkv_t = jnp.transpose(qkv_weight, (1, 2, 0))
    own_a = qkv_t[:2].reshape(2 * hw, d)
    own_b = jnp.concatenate([qkv_t[2], out_weight])
    pa, pb = gather(own_a, own_b)
    fa, fb = gather(up_weight, down_weight)
    gs = to_clip(cotangent)
    r = lambda v: v.reshape(1, d)

    start, n1, qkv, mixed, lse, middle, n2, w = attn_fwd(
        n, nz, idx, xs, proj_weight, proj_bias[:, None, :], r(ln1_gain), r(ln1_bias), own_a, own_b, bq,
        r(out_bias), r(ln2_gain), r(ln2_bias), pa, pb)
    out, mid_grad, mid_low, keep_u, send_u, keep_d, send_d, dub, sums2 = ffn(
        n, nz, idx, gs, n2, middle, up_weight, down_weight, up_bias.reshape(nz, 1, f), r(down_bias),
        r(ln2_gain), fa, fb)
    keep_a, send_a, keep_b, send_b, dqv, tok_grad, sums1 = attn_bwd(
        n, nz, idx, xs, mid_low, mid_grad, start, n1, proj_weight, r(ln1_gain), w, qkv, mixed, lse)

    up_z, down_z = over_z(fold(keep_u, send_u, False), fold(keep_d, send_d, True))
    output = to_rows(out, BF16)
    up_g, down_g = share(up_z, down_z, (d // n, f // n))

    tokens_grad = to_rows(tok_grad, F32)
    a_z, b_z = over_z(fold(keep_a, send_a, False), fold(keep_b, send_b, True))
    ra = 2 * hw // n
    tail = b_z[ra:]
    b_all = jnp.concatenate([b_z[:ra], tail] + [shift(tail, s) for s in range(1, nz)])
    a_g, b_g, proj_g = share(a_z, b_all, (ra, ra, tail.shape[0]))

    is_patch = idx[0] == 1
    bias_pair = jnp.stack([jnp.where(is_patch, 0.0, sums1[0]), jnp.where(is_patch, sums1[0], 0.0)])
    dqv_cols = dqv.reshape(nz, 3, hw)
    small = jnp.concatenate([
        bias_pair, sums1[1:3], sums2, dub.reshape(nz, f).reshape(-1, d),
        dqv_cols[:, 0].reshape(-1, d), dqv_cols[:, 2].reshape(-1, d)], axis=0)
    for k in range(nw.bit_length() - 1):
        small = small + swap(small, 1 << k)
    for k in range(nz.bit_length() - 1):
        small = small + lax.ppermute(small, "narrow", [(i, i ^ (1 << k)) for i in range(nz)])
    last = 8 + nz * f // d
    up_b = lax.dynamic_index_in_dim(small[8:last].reshape(nz, f), me_z, 0, keepdims=False)
    qv = lax.dynamic_slice_in_dim(small[last:].reshape(2, nz * hw), me_z * hw, hw, 1)
    a_g = a_g.reshape(2 * hw, d)
    b_g = b_g.reshape(2 * hw, d)
    qkv_g = jnp.transpose(jnp.concatenate([a_g, b_g[:hw]]).reshape(3, hw, d), (2, 0, 1))
    return (output, tokens_grad, proj_g.reshape(-1, feat, d), small[0:2], small[2], small[3], qkv_g, qv,
            b_g[hw:], small[6], small[4], small[5], up_g.reshape(d, f), up_b, down_g.reshape(f, d),
            small[7])


def solution(mesh):
    in_specs = (
        P("wide", "narrow", None), P("wide"), P(), P(), P(), P(), P(None, None, "narrow"),
        P(None, "narrow"), P("narrow", None), P(), P(), P(), P(None, "narrow"), P(),
        P("narrow", None), P(), P("wide", "narrow", None),
    )
    out_specs = (
        P("wide", "narrow", None), P("wide", "narrow", None), P(), P(), P(), P(),
        P(None, None, "narrow"), P(None, "narrow"), P("narrow", None), P(), P(), P(),
        P(None, "narrow"), P("narrow"), P("narrow", None), P(),
    )
    body = functools.partial(per_device, mesh.shape["wide"], mesh.shape["narrow"])

    return jax.shard_map(body, mesh=mesh, in_specs=in_specs, out_specs=out_specs, check_vma=False)
```

```python
import functools

import jax
import jax.numpy as jnp
from jax import lax
from jax.experimental import pallas as pl
from jax.experimental.pallas import tpu as pltpu
from jax.sharding import PartitionSpec as P


HEAD_DIM = 64
SCALE = HEAD_DIM ** (-0.5)
EPS = 1e-06
F32 = jnp.float32
BF16 = jnp.bfloat16
NN = (((1,), (0,)), ((), ()))
NT = (((1,), (1,)), ((), ()))
TN = (((0,), (0,)), ((), ()))


def dot(a, b, dims):
    return lax.dot_general(a, b, dims, preferred_element_type=F32)


def row_stats(v):
    mean = jnp.mean(v, axis=-1, keepdims=True)
    cen = v - mean
    var = jnp.mean(cen * cen, axis=-1, keepdims=True)
    return cen, lax.rsqrt(var + EPS)


def norm_back(v, grad, gain):
    cen, r = row_stats(v)
    xhat = cen * r
    q = grad * gain
    mq = jnp.mean(q, axis=-1, keepdims=True)
    mqx = jnp.mean(q * xhat, axis=-1, keepdims=True)
    return r * (q - mq - xhat * mqx), xhat


def gelu_pair(u):
    phi = 0.5 * (1.0 + lax.erf(u * (2.0 ** -0.5)))
    dens = jnp.exp(-0.5 * u * u) * 0.3989422804014327
    return u * phi, phi + u * dens


def rows_of(i, size):
    start = i * size
    return pl.ds(pl.multiple_of(start, size & -size), size)


def step_bits(n, flip):
    bits = [1 << k for k in range(1, n.bit_length() - 1)]
    return bits[::-1] if flip else bits


def kept(n, flip):
    order = [0]
    for b in step_bits(n, flip)[::-1]:
        order = order + [r | b for r in order]
    return order


def spread_order(n, flip):
    bits = step_bits(n, flip)[::-1]
    sets = [[0]]
    for b in bits:
        now = [r for one in sets for r in one]
        sets = [now, [r ^ b for r in now]]
    return sets + [[r ^ 1 for r in one] for one in sets]


def put_pieces(dst, base, bufs, me, n, flip):
    for ref, rs in zip(bufs, spread_order(n, flip)):
        size = ref.shape[2]
        for i, r in enumerate(rs):
            dst[rows_of(base // size + (me ^ r), size), :] = ref[i, 0]


def cut_pieces(src, base, keep, send, me, n, flip, size, at=None):
    for i, r in enumerate(kept(n, flip)):
        for ref, q in ((keep, r), (send, r | 1)):
            val = src[rows_of(base // size + (me ^ q), size), :]
            if at is None:
                ref[i, 0] = val
            else:
                ref[i, at, 0:size] = val


def attn_fwd_kernel(n, nbuf, idx, *refs):
    xs, refs = refs[:nbuf[0]], refs[nbuf[0]:]
    proj, pbias, g1, b1, own_a, own_b, bq, ob, g2, b2 = refs[:10]
    refs = refs[10:]
    pa, pb, refs = refs[:nbuf[1]], refs[nbuf[1]:2 * nbuf[1]], refs[2 * nbuf[1]:]
    start, n1, qkv, mixed, lse, middle, n2, w, xfull = refs
    z = pl.program_id(0)
    nz = pl.num_programs(0)
    me = idx[1]
    half = own_a.shape[0]

    @pl.when(z == 0)
    def _():
        part_rows = xs[0].shape[0]
        for s, ref in enumerate(xs):
            xfull[rows_of(lax.rem(idx[2] - s + len(xs), len(xs)), part_rows), :] = ref[...]
        s = dot(xfull[...], proj[0], NN) + pbias[0]
        start[...] = s
        middle[...] = s + ob[...]
        cen, r = row_stats(s)
        n1[...] = (cen * r * g1[...] + b1[...]).astype(BF16)
        w[0, 0:half, :] = own_a[...]
        w[0, half:2 * half, :] = own_b[...]

    @pl.when(z > 0)
    def _():
        put_pieces(w.at[0], 0, pa, me, n, False)
        put_pieces(w.at[0], half, pb, me, n, True)

    width = mixed.shape[1]
    qkv[0] = (dot(w[0, 0:3 * width, :], n1[...], NT) + bq[0]).astype(BF16)
    for h in range(width // HEAD_DIM):
        lo = h * HEAD_DIM
        q_t = qkv[0, lo:lo + HEAD_DIM, :]
        k_t = qkv[0, width + lo:width + lo + HEAD_DIM, :]
        v_t = qkv[0, 2 * width + lo:2 * width + lo + HEAD_DIM, :]
        s = dot(k_t, q_t, TN) * SCALE
        top = jnp.max(s, axis=0, keepdims=True)
        e = jnp.exp(s - top)
        total = jnp.sum(e, axis=0, keepdims=True)
        p = (e * (1.0 / total)).astype(BF16)
        lse[0, h:h + 1, :] = top + jnp.log(total)
        mixed[0, lo:lo + HEAD_DIM, :] = dot(v_t, p, NN).astype(BF16)
    middle[...] += dot(mixed[0], w[0, 3 * width:4 * width, :], TN)

    @pl.when(z == nz - 1)
    def _():
        cen, r = row_stats(middle[...])
        n2[...] = (cen * r * g2[...] + b2[...]).astype(BF16)


def ffn_kernel(n, nbuf, idx, *refs):
    gs, refs = refs[:nbuf[0]], refs[nbuf[0]:]
    n2, middle, own_up, own_down, ub, db, g2 = refs[:7]
    refs = refs[7:]
    pa, pb, refs = refs[:nbuf[1]], refs[nbuf[1]:2 * nbuf[1]], refs[2 * nbuf[1]:]
    out, mid_grad, mid_low, keep_u, send_u, keep_d, send_d, dub, sums = refs[:9]
    acc, dn2, n2t, g, up, down, gup, gdown = refs[9:]
    z = pl.program_id(0)
    nz = pl.num_programs(0)
    me = idx[1]
    num = len(gs)

    @pl.when(z == 0)
    def _():
        part_rows = gs[0].shape[0]
        for s, ref in enumerate(gs):
            g[rows_of(lax.rem(idx[2] - s + num, num), part_rows), :] = ref[...]
        acc[...] = middle[...] + db[...]
        dn2[...] = jnp.zeros_like(dn2)
        n2t[...] = n2[...].T
        up[...] = own_up[...]
        down[...] = own_down[...]

    @pl.when(z > 0)
    def _():
        put_pieces(up, 0, pa, me, n, False)
        put_pieces(down, 0, pb, me, n, True)

    u = dot(n2[...], up[...], NN) + ub[0]
    h, slope = gelu_pair(u)
    h = h.astype(BF16)
    acc[...] += dot(h, down[...], NN)
    gdown[...] = dot(h, g[...], TN).astype(BF16)
    pre = (dot(g[...], down[...], NT) * slope).astype(BF16)
    dub[0] = jnp.sum(pre.astype(F32), axis=0, keepdims=True)
    gup[...] = dot(n2t[...], pre, NN).astype(BF16)
    dn2[...] += dot(pre, up[...], NT)
    cut_pieces(gup, 0, keep_u, send_u, me, n, False, gup.shape[0] // n)
    cut_pieces(gdown, 0, keep_d, send_d, me, n, True, gdown.shape[0] // n)

    @pl.when(z == nz - 1)
    def _():
        part_rows = gs[0].shape[0]
        for s in range(num):
            block = rows_of(lax.rem(idx[2] + s, num), part_rows)
            out[s] = acc[block, :].astype(BF16)
        gf = g[...].astype(F32)
        d = dn2[...]
        back, xhat = norm_back(middle[...], d, g2[...])
        mg = gf + back
        mid_grad[...] = mg
        ml = mg.astype(BF16)
        mid_low[...] = ml
        sums[...] = jnp.concatenate([
            jnp.sum(d * xhat, axis=0, keepdims=True),
            jnp.sum(d, axis=0, keepdims=True),
            jnp.sum(ml.astype(F32), axis=0, keepdims=True),
            jnp.sum(gf, axis=0, keepdims=True),
        ], axis=0)


def attn_bwd_kernel(n, nbuf, idx, *refs):
    xs, refs = refs[:nbuf[0]], refs[nbuf[0]:]
    mid_low, mid_grad, start, n1, proj, g1, w, qkv, mixed, lse, sums2, dub = refs[:12]
    keep_a, send_a, keep_b, send_b, tok_grad, small = refs[12:18]
    dn1, dqkv, gw, xfull, pair, tok = refs[18:]
    z = pl.program_id(0)
    nz = pl.num_programs(0)
    me = idx[1]
    num = len(xs)

    @pl.when(z == 0)
    def _():
        dn1[...] = jnp.zeros_like(dn1)
        small[...] = jnp.zeros_like(small)
        small[4:8, :] = sums2[...]
        for s in range(num):
            small[8 + s:9 + s, :] = dub[s]

    ml = mid_low[...]
    width = mixed.shape[1]
    gw[3 * width:4 * width, :] = dot(mixed[0], ml, NN).astype(BF16)
    do_all = dot(w[0, 3 * width:4 * width, :], ml, NT).astype(BF16)
    for h in range(width // HEAD_DIM):
        lo = h * HEAD_DIM
        q_t = qkv[0, lo:lo + HEAD_DIM, :]
        k_t = qkv[0, width + lo:width + lo + HEAD_DIM, :]
        v_t = qkv[0, 2 * width + lo:2 * width + lo + HEAD_DIM, :]
        do_t = do_all[lo:lo + HEAD_DIM, :]
        p = jnp.exp(dot(k_t, q_t, TN) * SCALE - lse[0, h:h + 1, :])
        dp = dot(v_t, do_t, TN)
        dsum = jnp.sum(p * dp, axis=0, keepdims=True)
        ds = (p * (dp - dsum)).astype(BF16)
        dqkv[lo:lo + HEAD_DIM, :] = (dot(k_t, ds, NN) * SCALE).astype(BF16)
        dqkv[width + lo:width + lo + HEAD_DIM, :] = (dot(q_t, ds, NT) * SCALE).astype(BF16)
        dqkv[2 * width + lo:2 * width + lo + HEAD_DIM, :] = dot(do_t, p.astype(BF16), NT).astype(BF16)
    dw = dqkv[...]
    ones = jnp.ones((8, dw.shape[1]), BF16)
    small[pl.ds(8 + num + lax.rem(idx[2] - z + num, num), 1), 0:3 * width] = dot(ones, dw, NT)[0:1, :]
    gw[0:3 * width, :] = dot(dw, n1[...], NN).astype(BF16)
    dn1[...] += dot(dw, w[0, 0:3 * width, :], TN)
    half = 2 * width
    cut_pieces(gw, 0, keep_a, send_a, me, n, False, half // n)
    cut_pieces(gw, half, keep_b, send_b, me, n, True, half // n, at=z)

    @pl.when(z == nz - 1)
    def _():
        part_rows = xs[0].shape[0]
        for s, ref in enumerate(xs):
            xfull[rows_of(lax.rem(idx[2] - s + num, num), part_rows), :] = ref[...]
        d = dn1[...]
        back, xhat = norm_back(start[...], d, g1[...])
        sl = (mid_grad[...] + back).astype(BF16)
        tok[...] = dot(sl, proj[0], NT).astype(BF16)
        for s in range(num):
            tok_grad[s] = tok[rows_of(lax.rem(idx[2] + s, num), part_rows), :]
        feat = proj.shape[1]
        pair[rows_of(idx[0], feat), :] = dot(xfull[...], sl, TN).astype(BF16)
        pair[rows_of(1 - idx[0], feat), :] = jnp.zeros((feat, sl.shape[1]), BF16)
        tail = pair.shape[0] // (num * n)
        for i, r in enumerate(kept(n, True)):
            for s in range(num):
                zz = lax.rem(idx[2] - s + num, num)
                for ref, q in ((keep_b, r), (send_b, r | 1)):
                    ref[i, s, half // n:half // n + tail, :] = pair[rows_of(zz * n + (me ^ q), tail), :]
        small[pl.ds(idx[0], 1), :] = jnp.sum(sl.astype(F32), axis=0, keepdims=True)
        small[2:3, :] = jnp.sum(d * xhat, axis=0, keepdims=True)
        small[3:4, :] = jnp.sum(d, axis=0, keepdims=True)


def place_kernel(n, sizes, nz, idx, lo, hi, a, b, *c):
    me = idx[1]
    ra, rb = sizes[:2]
    for flip, ref, at, size in ((False, a, 0, ra), (True, b, ra, rb)):
        for i, r in enumerate(kept(n, flip)):
            for src, q in ((lo, r), (hi, r | 1)):
                ref[me ^ q] = src[i, at:at + size, :].astype(F32)
                if c and flip:
                    for s in range(nz):
                        first = ra + rb + s * sizes[2]
                        zz = lax.rem(idx[2] - s + nz, nz)
                        c[0][zz * n + (me ^ q)] = src[i, first:first + sizes[2], :].astype(F32)


def whole(shape):
    return pl.BlockSpec(shape, lambda z, *_: (0,) * len(shape))


def part(shape):
    return pl.BlockSpec((1,) + shape, lambda z, *_: (z,) + (0,) * len(shape))


def true_part(shape, nz):
    return pl.BlockSpec((1,) + shape, lambda z, k: (lax.rem(k[2] - z + nz, nz),) + (0,) * len(shape))


def by_kind(shape):
    return pl.BlockSpec((1,) + shape, lambda z, k: (k[0],) + (0,) * len(shape))


def piece_in(v):
    k, _, r, d = v.shape
    return pl.BlockSpec((k, 1, r, d), lambda z, *_: (0, jnp.maximum(z - 1, 0), 0, 0))


def piece_out(k, r, d):
    return pl.BlockSpec((k, 1, r, d), lambda z, *_: (0, z, 0, 0))


def sds(shape, dtype):
    return jax.ShapeDtypeStruct(shape, dtype)


PARAMS = pltpu.CompilerParams(dimension_semantics=("arbitrary",), vmem_limit_bytes=58 << 20)


def work(us):
    return us * 10 ** 9, us * 10 ** 6, 0


def call(kernel, grid, args, in_specs, outs, scratch, cost=(0, 0, 0)):
    estimate = pl.CostEstimate(flops=cost[0], bytes_accessed=cost[1], transcendentals=cost[2])
    return pl.pallas_call(
        kernel,
        grid_spec=pltpu.PrefetchScalarGridSpec(
            num_scalar_prefetch=1, grid=grid, in_specs=in_specs, out_specs=[s for s, _ in outs],
            scratch_shapes=scratch),
        out_shape=[o for _, o in outs], compiler_params=PARAMS, cost_estimate=estimate,
    )(*args)


def attn_fwd(n, nz, idx, xs, proj, pbias, g1, b1, own_a, own_b, bq, ob, g2, b2, pa, pb):
    rows, feat = xs[0].shape
    half, d = own_a.shape
    hw = half // 2
    seq = rows * nz
    row = (1, d)
    return call(
        functools.partial(attn_fwd_kernel, n, (nz, len(pa))), (nz,),
        (idx, *xs, proj, pbias, g1, b1, own_a, own_b, bq, ob, g2, b2, *pa, *pb),
        [whole((rows, feat))] * nz + [by_kind((feat, d)), by_kind(row), whole(row), whole(row),
                                      whole((half, d)), whole((half, d)), part((3 * hw, 1)),
                                      whole(row), whole(row), whole(row)]
        + [piece_in(v) for v in (*pa, *pb)],
        [(whole((seq, d)), sds((seq, d), F32)), (whole((seq, d)), sds((seq, d), BF16)),
         (part((3 * hw, seq)), sds((nz, 3 * hw, seq), BF16)), (part((hw, seq)), sds((nz, hw, seq), BF16)),
         (part((8, seq)), sds((nz, 8, seq), F32)), (whole((seq, d)), sds((seq, d), F32)),
         (whole((seq, d)), sds((seq, d), BF16)), (part((2 * half, d)), sds((nz, 2 * half, d), BF16))],
        [pltpu.VMEM((seq, feat), BF16)], work(20))


def ffn(n, nz, idx, gs, n2, middle, own_up, own_down, ub, db, g2, pa, pb):
    rows, d = gs[0].shape
    f = own_up.shape[1]
    seq = rows * nz
    row = (1, d)
    h = n // 2
    return call(
        functools.partial(ffn_kernel, n, (nz, len(pa))), (nz,),
        (idx, *gs, n2, middle, own_up, own_down, ub, db, g2, *pa, *pb),
        [whole((rows, d))] * nz + [whole((seq, d)), whole((seq, d)), whole((d, f)), whole((f, d)),
                                   true_part((1, f), nz), whole(row), whole(row)]
        + [piece_in(v) for v in (*pa, *pb)],
        [(whole((nz, rows, d)), sds((nz, rows, d), BF16)), (whole((seq, d)), sds((seq, d), F32)),
         (whole((seq, d)), sds((seq, d), BF16)),
         (piece_out(h, d // n, f), sds((h, nz, d // n, f), BF16)),
         (piece_out(h, d // n, f), sds((h, nz, d // n, f), BF16)),
         (piece_out(h, f // n, d), sds((h, nz, f // n, d), BF16)),
         (piece_out(h, f // n, d), sds((h, nz, f // n, d), BF16)),
         (true_part((1, f), nz), sds((nz, 1, f), F32)), (whole((4, d)), sds((4, d), F32))],
        [pltpu.VMEM((seq, d), F32), pltpu.VMEM((seq, d), F32), pltpu.VMEM((d, seq), BF16),
         pltpu.VMEM((seq, d), BF16), pltpu.VMEM((d, f), BF16), pltpu.VMEM((f, d), BF16),
         pltpu.VMEM((d, f), BF16), pltpu.VMEM((f, d), BF16)], work(26))


def attn_bwd(n, nz, idx, xs, mid_low, mid_grad, start, n1, proj, g1, w, qkv, mixed, lse, sums2, dub):
    rows, feat = xs[0].shape
    seq, d = n1.shape
    hw = mixed.shape[1]
    row = (1, d)
    h = n // 2
    ra = 2 * hw // n
    rb = ra + proj.shape[0] * feat // (nz * n)
    return call(
        functools.partial(attn_bwd_kernel, n, (nz,)), (nz,),
        (idx, *xs, mid_low, mid_grad, start, n1, proj, g1, w, qkv, mixed, lse, sums2, dub),
        [whole((rows, feat))] * nz + [whole((seq, d)), whole((seq, d)), whole((seq, d)), whole((seq, d)),
                                      by_kind((feat, d)), whole(row), part((4 * hw, d)),
                                      part((3 * hw, seq)), part((hw, seq)), part((8, seq)),
                                      whole((4, d)), whole((nz, 1, d))],
        [(piece_out(h, ra, d), sds((h, nz, ra, d), BF16)), (piece_out(h, ra, d), sds((h, nz, ra, d), BF16)),
         (whole((h, nz, rb, d)), sds((h, nz, rb, d), BF16)), (whole((h, nz, rb, d)), sds((h, nz, rb, d), BF16)),
         (whole((nz, rows, feat)), sds((nz, rows, feat), BF16)),
         (whole((8 + 2 * nz, d)), sds((8 + 2 * nz, d), F32))],
        [pltpu.VMEM((seq, d), F32), pltpu.VMEM((3 * hw, seq), BF16), pltpu.VMEM((4 * hw, d), BF16),
         pltpu.VMEM((seq, feat), BF16), pltpu.VMEM((proj.shape[0] * feat, d), BF16),
         pltpu.VMEM((seq, feat), BF16)], work(26))


def place(n, nz, idx, lo, hi, sizes):
    h, rows, d = lo.shape
    col = 256 if d % 256 == 0 else d
    outs = [(n, sizes[0]), (n, sizes[1])] + [(n * nz, s) for s in sizes[2:]]
    spec = lambda a, b: pl.BlockSpec((a, b, col), lambda j, *_: (0, 0, j))
    return call(
        functools.partial(place_kernel, n, sizes, nz), (d // col,), (idx, lo, hi), [spec(h, rows)] * 2,
        [(spec(a, b), sds((a, b, d), F32)) for a, b in outs], [], work(5))


def line_up_kernel(idx, *refs):
    num = len(refs) - 1
    for s, ref in enumerate(refs[:num]):
        refs[num][lax.rem(idx[2] - s + num, num)] = ref[...].astype(refs[num].dtype)


def line_up(nz, idx, blocks, dtype):
    rows, d = blocks[0].shape
    return call(
        line_up_kernel, (1,), (idx, *blocks), [whole((rows, d))] * nz,
        [(whole((nz, rows, d)), sds((nz, rows, d), dtype))], [], work(2))[0]


def per_device(nw, nz, tokens, kind, proj_weight, proj_bias, ln1_gain, ln1_bias, qkv_weight, qv_bias,
               out_weight, out_bias, ln2_gain, ln2_bias, up_weight, up_bias, down_weight, down_bias,
               cotangent):
    d, f = up_weight.shape
    hw = out_weight.shape[0]
    feat = tokens.shape[2]
    n = min(nw, 8)
    me_w = lax.axis_index("wide")
    me_z = lax.axis_index("narrow")
    me = lax.rem(me_w, n)
    my_kind = lax.dynamic_index_in_dim(kind, me_z, 0, keepdims=False)
    idx = jnp.stack([jnp.where(my_kind == 1, 1, 0), me, me_z]).astype(jnp.int32)

    def swap(v, bit):
        return lax.ppermute(v, "wide", [(i, i ^ bit) for i in range(nw)])

    def shift(v, s):
        return lax.ppermute(v, "narrow", [(i, (i + s) % nz) for i in range(nz)])

    def add(a, b):
        return (a.astype(F32) + b.astype(F32)).astype(BF16)

    def to_clip(v):
        return [lax.dynamic_index_in_dim(v, me_z, 0, keepdims=False)] + [
            shift(lax.dynamic_index_in_dim(v, lax.rem(me_z + s, nz), 0, keepdims=False), s)
            for s in range(1, nz)]

    def to_rows(v, dtype):
        return line_up(nz, idx, [v[0]] + [shift(v[s], s) for s in range(1, nz)], dtype)

    def spread(cur, flip, last):
        bufs = [cur]
        for b in step_bits(n, flip)[::-1]:
            now = jnp.concatenate(bufs) if len(bufs) > 1 else bufs[0]
            bufs = [now, swap(now, b)]
        if not last:
            return jnp.concatenate(bufs)
        return bufs + [swap(v, 1) for v in bufs]

    def gather(a, b):
        ra, rb = a.shape[0] // n, b.shape[0] // n
        mine = jnp.concatenate([lax.dynamic_slice_in_dim(a, me * ra, ra, 0),
                                lax.dynamic_slice_in_dim(b, me * rb, rb, 0)])
        got = jnp.stack([shift(mine, s) for s in range(1, nz)])
        return (spread(got[None, :, :ra], False, True),
                spread(got[None, :, ra:], True, True))

    def fold(keep, send, flip):
        got = swap(send, 1)
        for b in step_bits(n, flip):
            h = keep.shape[0] // 2
            go = add(keep[h:], got[h:])
            keep, got = add(keep[:h], got[:h]), swap(go, b)
        total = add(keep[0], got[0])
        for k in range(n.bit_length() - 1, nw.bit_length() - 1):
            total = add(total, swap(total, 1 << k))
        return total

    def over_z(a, b):
        ra = a.shape[1]
        total = [a[0].astype(F32), b[0].astype(F32)]
        for s in range(1, nz):
            both = jnp.concatenate([a[s], b[s]])
            got = shift(both, -s)
            total = [total[0] + got[:ra].astype(F32), total[1] + got[ra:].astype(F32)]
        return total[0].astype(BF16), total[1].astype(BF16)

    def share(a, b, sizes):
        lo = jnp.concatenate([spread(a[None], False, False),
                              spread(b[None], True, False)], axis=1)
        return place(n, nz, idx, lo, swap(lo, 1), sizes)

    xs = to_clip(tokens)
    bias_three = jnp.concatenate([qv_bias[0], jnp.zeros_like(qv_bias[0]), qv_bias[1]])
    bq = jnp.stack([bias_three] + [shift(bias_three, s) for s in range(1, nz)])[:, :, None]
    qkv_t = jnp.transpose(qkv_weight, (1, 2, 0))
    own_a = qkv_t[:2].reshape(2 * hw, d)
    own_b = jnp.concatenate([qkv_t[2], out_weight])
    pa, pb = gather(own_a, own_b)
    fa, fb = gather(up_weight, down_weight)
    gs = to_clip(cotangent)
    r = lambda v: v.reshape(1, d)

    start, n1, qkv, mixed, lse, middle, n2, w = attn_fwd(
        n, nz, idx, xs, proj_weight, proj_bias[:, None, :], r(ln1_gain), r(ln1_bias), own_a, own_b, bq,
        r(out_bias), r(ln2_gain), r(ln2_bias), pa, pb)
    out, mid_grad, mid_low, keep_u, send_u, keep_d, send_d, dub, sums2 = ffn(
        n, nz, idx, gs, n2, middle, up_weight, down_weight, up_bias.reshape(nz, 1, f), r(down_bias),
        r(ln2_gain), fa, fb)
    keep_a, send_a, keep_b, send_b, tok_grad, small = attn_bwd(
        n, nz, idx, xs, mid_low, mid_grad, start, n1, proj_weight, r(ln1_gain), w, qkv, mixed, lse,
        sums2, dub)

    up_z, down_z = over_z(fold(keep_u, send_u, False), fold(keep_d, send_d, True))
    output = to_rows(out, BF16)
    up_g, down_g = share(up_z, down_z, (d // n, f // n))

    tokens_grad = to_rows(tok_grad, F32)
    a_z, b_z = over_z(fold(keep_a, send_a, False), fold(keep_b, send_b, True))
    ra = 2 * hw // n
    tail = b_z[ra:]
    b_all = jnp.concatenate([b_z[:ra], tail] + [shift(tail, s) for s in range(1, nz)])
    a_g, b_g, proj_g = share(a_z, b_all, (ra, ra, tail.shape[0]))

    for k in range(nw.bit_length() - 1):
        small = small + swap(small, 1 << k)
    for k in range(nz.bit_length() - 1):
        small = small + lax.ppermute(small, "narrow", [(i, i ^ (1 << k)) for i in range(nz)])
    up_b = lax.dynamic_index_in_dim(small, 8 + me_z, 0, keepdims=False)
    dqv = lax.dynamic_index_in_dim(small, 8 + nz + me_z, 0, keepdims=False)
    qv = jnp.stack([dqv[:hw], dqv[2 * hw:3 * hw]])
    a_g = a_g.reshape(2 * hw, d)
    b_g = b_g.reshape(2 * hw, d)
    qkv_g = jnp.transpose(jnp.concatenate([a_g, b_g[:hw]]).reshape(3, hw, d), (2, 0, 1))
    return (output, tokens_grad, proj_g.reshape(-1, feat, d), small[0:2], small[2], small[3], qkv_g, qv,
            b_g[hw:], small[6], small[4], small[5], up_g.reshape(d, f), up_b, down_g.reshape(f, d),
            small[7])


def solution(mesh):
    in_specs = (
        P("wide", "narrow", None), P("wide"), P(), P(), P(), P(), P(None, None, "narrow"),
        P(None, "narrow"), P("narrow", None), P(), P(), P(), P(None, "narrow"), P(),
        P("narrow", None), P(), P("wide", "narrow", None),
    )
    out_specs = (
        P("wide", "narrow", None), P("wide", "narrow", None), P(), P(), P(), P(),
        P(None, None, "narrow"), P(None, "narrow"), P("narrow", None), P(), P(), P(),
        P(None, "narrow"), P("narrow"), P("narrow", None), P(),
    )
    body = functools.partial(per_device, mesh.shape["wide"], mesh.shape["narrow"])

    return jax.shard_map(body, mesh=mesh, in_specs=in_specs, out_specs=out_specs, check_vma=False)
```

```python
import functools

import jax
import jax.numpy as jnp
from jax import lax
from jax.experimental import pallas as pl
from jax.experimental.pallas import tpu as pltpu
from jax.sharding import PartitionSpec as P


HEAD_DIM = 64
SCALE = HEAD_DIM ** (-0.5)
EPS = 1e-06
F32 = jnp.float32
BF16 = jnp.bfloat16
NN = (((1,), (0,)), ((), ()))
NT = (((1,), (1,)), ((), ()))
TN = (((0,), (0,)), ((), ()))


def dot(a, b, dims):
    return lax.dot_general(a, b, dims, preferred_element_type=F32)


def row_stats(v):
    mean = jnp.mean(v, axis=-1, keepdims=True)
    cen = v - mean
    var = jnp.mean(cen * cen, axis=-1, keepdims=True)
    return cen, lax.rsqrt(var + EPS)


def norm_back(v, grad, gain):
    cen, r = row_stats(v)
    xhat = cen * r
    q = grad * gain
    mq = jnp.mean(q, axis=-1, keepdims=True)
    mqx = jnp.mean(q * xhat, axis=-1, keepdims=True)
    return r * (q - mq - xhat * mqx), xhat


def gelu_pair(u):
    phi = 0.5 * (1.0 + lax.erf(u * (2.0 ** -0.5)))
    dens = jnp.exp(-0.5 * u * u) * 0.3989422804014327
    return u * phi, phi + u * dens


def rows_of(i, size):
    start = i * size
    return pl.ds(pl.multiple_of(start, size & -size), size)


def step_bits(n, flip):
    bits = [1 << k for k in range(1, n.bit_length() - 1)]
    return bits[::-1] if flip else bits


def kept(n, flip):
    order = [0]
    for b in step_bits(n, flip)[::-1]:
        order = order + [r | b for r in order]
    return order


def spread_order(n, flip):
    bits = step_bits(n, flip)[::-1]
    sets = [[0]]
    for b in bits:
        now = [r for one in sets for r in one]
        sets = [now, [r ^ b for r in now]]
    return sets + [[r ^ 1 for r in one] for one in sets]


def put_pieces(dst, base, bufs, me, n, flip):
    for ref, rs in zip(bufs, spread_order(n, flip)):
        size = ref.shape[2]
        for i, r in enumerate(rs):
            dst[rows_of(base // size + (me ^ r), size), :] = ref[i, 0]


def cut_pieces(src, base, keep, send, me, n, flip, size, at=None):
    for i, r in enumerate(kept(n, flip)):
        for ref, q in ((keep, r), (send, r | 1)):
            val = src[rows_of(base // size + (me ^ q), size), :]
            if at is None:
                ref[i, 0] = val
            else:
                ref[i, at, 0:size] = val


def attn_fwd_kernel(n, nbuf, idx, *refs):
    xs, refs = refs[:nbuf[0]], refs[nbuf[0]:]
    proj, pbias, g1, b1, own_a, own_b, bq, ob, g2, b2 = refs[:10]
    refs = refs[10:]
    pa, pb, refs = refs[:nbuf[1]], refs[nbuf[1]:2 * nbuf[1]], refs[2 * nbuf[1]:]
    start, n1, qkv, mixed, lse, middle, n2, w, xfull = refs
    z = pl.program_id(0)
    nz = pl.num_programs(0)
    me = idx[1]
    half = own_a.shape[0]

    @pl.when(z == 0)
    def _():
        part_rows = xs[0].shape[0]
        for s, ref in enumerate(xs):
            xfull[rows_of(lax.rem(idx[2] - s + len(xs), len(xs)), part_rows), :] = ref[...]
        s = dot(xfull[...], proj[0], NN) + pbias[0]
        start[...] = s
        middle[...] = s + ob[...]
        cen, r = row_stats(s)
        n1[...] = (cen * r * g1[...] + b1[...]).astype(BF16)
        w[0, 0:half, :] = own_a[...]
        w[0, half:2 * half, :] = own_b[...]

    @pl.when(z > 0)
    def _():
        put_pieces(w.at[0], 0, pa, me, n, False)
        put_pieces(w.at[0], half, pb, me, n, True)

    width = mixed.shape[1]
    qkv[0] = (dot(w[0, 0:3 * width, :], n1[...], NT) + bq[0]).astype(BF16)
    for h in range(width // HEAD_DIM):
        lo = h * HEAD_DIM
        q_t = qkv[0, lo:lo + HEAD_DIM, :]
        k_t = qkv[0, width + lo:width + lo + HEAD_DIM, :]
        v_t = qkv[0, 2 * width + lo:2 * width + lo + HEAD_DIM, :]
        s = dot(k_t, q_t, TN) * SCALE
        top = jnp.max(s, axis=0, keepdims=True)
        e = jnp.exp(s - top)
        total = jnp.sum(e, axis=0, keepdims=True)
        p = (e * (1.0 / total)).astype(BF16)
        lse[0, h:h + 1, :] = top + jnp.log(total)
        mixed[0, lo:lo + HEAD_DIM, :] = dot(v_t, p, NN).astype(BF16)
    middle[...] += dot(mixed[0], w[0, 3 * width:4 * width, :], TN)

    @pl.when(z == nz - 1)
    def _():
        cen, r = row_stats(middle[...])
        n2[...] = (cen * r * g2[...] + b2[...]).astype(BF16)


def ffn_kernel(n, nbuf, idx, *refs):
    gs, refs = refs[:nbuf[0]], refs[nbuf[0]:]
    n2, middle, own_up, own_down, ub, db, g2 = refs[:7]
    refs = refs[7:]
    pa, pb, refs = refs[:nbuf[1]], refs[nbuf[1]:2 * nbuf[1]], refs[2 * nbuf[1]:]
    out, mid_grad, mid_low, keep_u, send_u, keep_d, send_d, dub, sums = refs[:9]
    acc, dn2, n2t, g, up, down, gup, gdown = refs[9:]
    z = pl.program_id(0)
    nz = pl.num_programs(0)
    me = idx[1]
    num = len(gs)

    @pl.when(z == 0)
    def _():
        part_rows = gs[0].shape[0]
        for s, ref in enumerate(gs):
            g[rows_of(lax.rem(idx[2] - s + num, num), part_rows), :] = ref[...]
        acc[...] = middle[...] + db[...]
        dn2[...] = jnp.zeros_like(dn2)
        n2t[...] = n2[...].T
        up[...] = own_up[...]
        down[...] = own_down[...]

    @pl.when(z > 0)
    def _():
        put_pieces(up, 0, pa, me, n, False)
        put_pieces(down, 0, pb, me, n, True)

    u = dot(n2[...], up[...], NN) + ub[0]
    h, slope = gelu_pair(u)
    h = h.astype(BF16)
    acc[...] += dot(h, down[...], NN)
    gdown[...] = dot(h, g[...], TN).astype(BF16)
    pre = (dot(g[...], down[...], NT) * slope).astype(BF16)
    dub[0] = jnp.sum(pre.astype(F32), axis=0, keepdims=True)
    gup[...] = dot(n2t[...], pre, NN).astype(BF16)
    dn2[...] += dot(pre, up[...], NT)
    cut_pieces(gup, 0, keep_u, send_u, me, n, False, gup.shape[0] // n)
    cut_pieces(gdown, 0, keep_d, send_d, me, n, True, gdown.shape[0] // n)

    @pl.when(z == nz - 1)
    def _():
        part_rows = gs[0].shape[0]
        for s in range(num):
            block = rows_of(lax.rem(idx[2] + s, num), part_rows)
            out[s] = acc[block, :].astype(BF16)
        gf = g[...].astype(F32)
        d = dn2[...]
        back, xhat = norm_back(middle[...], d, g2[...])
        mg = gf + back
        mid_grad[...] = mg
        ml = mg.astype(BF16)
        mid_low[...] = ml
        sums[...] = jnp.concatenate([
            jnp.sum(d * xhat, axis=0, keepdims=True),
            jnp.sum(d, axis=0, keepdims=True),
            jnp.sum(ml.astype(F32), axis=0, keepdims=True),
            jnp.sum(gf, axis=0, keepdims=True),
        ], axis=0)


def attn_bwd_kernel(n, nbuf, idx, *refs):
    xs, refs = refs[:nbuf[0]], refs[nbuf[0]:]
    mid_low, mid_grad, start, n1, proj, g1, w, qkv, mixed, lse, sums2, dub = refs[:12]
    keep_a, send_a, keep_b, send_b, tok_grad, small = refs[12:18]
    dn1, dqkv, gw, xfull, pair, tok = refs[18:]
    z = pl.program_id(0)
    nz = pl.num_programs(0)
    me = idx[1]
    num = len(xs)

    @pl.when(z == 0)
    def _():
        dn1[...] = jnp.zeros_like(dn1)
        small[...] = jnp.zeros_like(small)
        small[4:8, :] = sums2[...]
        for s in range(num):
            small[8 + s:9 + s, :] = dub[s]

    ml = mid_low[...]
    width = mixed.shape[1]
    gw[3 * width:4 * width, :] = dot(mixed[0], ml, NN).astype(BF16)
    do_all = dot(w[0, 3 * width:4 * width, :], ml, NT).astype(BF16)
    for h in range(width // HEAD_DIM):
        lo = h * HEAD_DIM
        q_t = qkv[0, lo:lo + HEAD_DIM, :]
        k_t = qkv[0, width + lo:width + lo + HEAD_DIM, :]
        v_t = qkv[0, 2 * width + lo:2 * width + lo + HEAD_DIM, :]
        do_t = do_all[lo:lo + HEAD_DIM, :]
        p = jnp.exp(dot(k_t, q_t, TN) * SCALE - lse[0, h:h + 1, :])
        dp = dot(v_t, do_t, TN)
        dsum = jnp.sum(p * dp, axis=0, keepdims=True)
        ds = (p * (dp - dsum)).astype(BF16)
        dqkv[lo:lo + HEAD_DIM, :] = (dot(k_t, ds, NN) * SCALE).astype(BF16)
        dqkv[width + lo:width + lo + HEAD_DIM, :] = (dot(q_t, ds, NT) * SCALE).astype(BF16)
        dqkv[2 * width + lo:2 * width + lo + HEAD_DIM, :] = dot(do_t, p.astype(BF16), NT).astype(BF16)
    dw = dqkv[...]
    ones = jnp.ones((8, dw.shape[1]), BF16)
    small[pl.ds(8 + num + lax.rem(idx[2] - z + num, num), 1), 0:3 * width] = dot(ones, dw, NT)[0:1, :]
    gw[0:3 * width, :] = dot(dw, n1[...], NN).astype(BF16)
    dn1[...] += dot(dw, w[0, 0:3 * width, :], TN)
    half = 2 * width
    cut_pieces(gw, 0, keep_a, send_a, me, n, False, half // n)
    cut_pieces(gw, half, keep_b, send_b, me, n, True, half // n, at=z)

    @pl.when(z == nz - 1)
    def _():
        part_rows = xs[0].shape[0]
        for s, ref in enumerate(xs):
            xfull[rows_of(lax.rem(idx[2] - s + num, num), part_rows), :] = ref[...]
        d = dn1[...]
        back, xhat = norm_back(start[...], d, g1[...])
        sl = (mid_grad[...] + back).astype(BF16)
        tok[...] = dot(sl, proj[0], NT).astype(BF16)
        for s in range(num):
            tok_grad[s] = tok[rows_of(lax.rem(idx[2] + s, num), part_rows), :]
        feat = proj.shape[1]
        pair[rows_of(idx[0], feat), :] = dot(xfull[...], sl, TN).astype(BF16)
        pair[rows_of(1 - idx[0], feat), :] = jnp.zeros((feat, sl.shape[1]), BF16)
        tail = pair.shape[0] // (num * n)
        for i, r in enumerate(kept(n, True)):
            for s in range(num):
                zz = lax.rem(idx[2] - s + num, num)
                for ref, q in ((keep_b, r), (send_b, r | 1)):
                    ref[i, s, half // n:half // n + tail, :] = pair[rows_of(zz * n + (me ^ q), tail), :]
        small[pl.ds(idx[0], 1), :] = jnp.sum(sl.astype(F32), axis=0, keepdims=True)
        small[2:3, :] = jnp.sum(d * xhat, axis=0, keepdims=True)
        small[3:4, :] = jnp.sum(d, axis=0, keepdims=True)


def place_kernel(n, sizes, nz, idx, lo, hi, a, b, *c):
    me = idx[1]
    ra, rb = sizes[:2]
    h = n // 2
    for src, off in ((lo, 0), (hi, 1)):
        for i, r in enumerate(kept(n, False)):
            a[me ^ (r | off)] = src[i, 0:ra, :].astype(F32)
        for i, r in enumerate(kept(n, True)):
            p = me ^ (r | off)
            val = src[i, ra:ra + rb, :].astype(F32)
            if not c:
                b[p] = val
                continue

            @pl.when(p < h)
            def _():
                a[n + p] = val

            @pl.when(p >= h)
            def _():
                b[p - h] = val

            for s in range(nz):
                first = ra + rb + s * sizes[2]
                zz = lax.rem(idx[2] - s + nz, nz)
                c[0][zz * n + p] = src[i, first:first + sizes[2], :].astype(F32)


def whole(shape):
    return pl.BlockSpec(shape, lambda z, *_: (0,) * len(shape))


def part(shape):
    return pl.BlockSpec((1,) + shape, lambda z, *_: (z,) + (0,) * len(shape))


def true_part(shape, nz):
    return pl.BlockSpec((1,) + shape, lambda z, k: (lax.rem(k[2] - z + nz, nz),) + (0,) * len(shape))


def by_kind(shape):
    return pl.BlockSpec((1,) + shape, lambda z, k: (k[0],) + (0,) * len(shape))


def piece_in(v):
    k, _, r, d = v.shape
    return pl.BlockSpec((k, 1, r, d), lambda z, *_: (0, jnp.maximum(z - 1, 0), 0, 0))


def piece_out(k, r, d):
    return pl.BlockSpec((k, 1, r, d), lambda z, *_: (0, z, 0, 0))


def sds(shape, dtype):
    return jax.ShapeDtypeStruct(shape, dtype)


PARAMS = pltpu.CompilerParams(dimension_semantics=("arbitrary",), vmem_limit_bytes=58 << 20)


def work(us):
    return us * 10 ** 9, us * 10 ** 6, 0


def call(kernel, grid, args, in_specs, outs, scratch, cost=(0, 0, 0)):
    estimate = pl.CostEstimate(flops=cost[0], bytes_accessed=cost[1], transcendentals=cost[2])
    return pl.pallas_call(
        kernel,
        grid_spec=pltpu.PrefetchScalarGridSpec(
            num_scalar_prefetch=1, grid=grid, in_specs=in_specs, out_specs=[s for s, _ in outs],
            scratch_shapes=scratch),
        out_shape=[o for _, o in outs], compiler_params=PARAMS, cost_estimate=estimate,
    )(*args)


def attn_fwd(n, nz, idx, xs, proj, pbias, g1, b1, own_a, own_b, bq, ob, g2, b2, pa, pb):
    rows, feat = xs[0].shape
    half, d = own_a.shape
    hw = half // 2
    seq = rows * nz
    row = (1, d)
    return call(
        functools.partial(attn_fwd_kernel, n, (nz, len(pa))), (nz,),
        (idx, *xs, proj, pbias, g1, b1, own_a, own_b, bq, ob, g2, b2, *pa, *pb),
        [whole((rows, feat))] * nz + [by_kind((feat, d)), by_kind(row), whole(row), whole(row),
                                      whole((half, d)), whole((half, d)), part((3 * hw, 1)),
                                      whole(row), whole(row), whole(row)]
        + [piece_in(v) for v in (*pa, *pb)],
        [(whole((seq, d)), sds((seq, d), F32)), (whole((seq, d)), sds((seq, d), BF16)),
         (part((3 * hw, seq)), sds((nz, 3 * hw, seq), BF16)), (part((hw, seq)), sds((nz, hw, seq), BF16)),
         (part((8, seq)), sds((nz, 8, seq), F32)), (whole((seq, d)), sds((seq, d), F32)),
         (whole((seq, d)), sds((seq, d), BF16)), (part((2 * half, d)), sds((nz, 2 * half, d), BF16))],
        [pltpu.VMEM((seq, feat), BF16)], work(20))


def ffn(n, nz, idx, gs, n2, middle, own_up, own_down, ub, db, g2, pa, pb):
    rows, d = gs[0].shape
    f = own_up.shape[1]
    seq = rows * nz
    row = (1, d)
    h = n // 2
    return call(
        functools.partial(ffn_kernel, n, (nz, len(pa))), (nz,),
        (idx, *gs, n2, middle, own_up, own_down, ub, db, g2, *pa, *pb),
        [whole((rows, d))] * nz + [whole((seq, d)), whole((seq, d)), whole((d, f)), whole((f, d)),
                                   true_part((1, f), nz), whole(row), whole(row)]
        + [piece_in(v) for v in (*pa, *pb)],
        [(whole((nz, rows, d)), sds((nz, rows, d), BF16)), (whole((seq, d)), sds((seq, d), F32)),
         (whole((seq, d)), sds((seq, d), BF16)),
         (piece_out(h, d // n, f), sds((h, nz, d // n, f), BF16)),
         (piece_out(h, d // n, f), sds((h, nz, d // n, f), BF16)),
         (piece_out(h, f // n, d), sds((h, nz, f // n, d), BF16)),
         (piece_out(h, f // n, d), sds((h, nz, f // n, d), BF16)),
         (true_part((1, f), nz), sds((nz, 1, f), F32)), (whole((4, d)), sds((4, d), F32))],
        [pltpu.VMEM((seq, d), F32), pltpu.VMEM((seq, d), F32), pltpu.VMEM((d, seq), BF16),
         pltpu.VMEM((seq, d), BF16), pltpu.VMEM((d, f), BF16), pltpu.VMEM((f, d), BF16),
         pltpu.VMEM((d, f), BF16), pltpu.VMEM((f, d), BF16)], work(26))


def attn_bwd(n, nz, idx, xs, mid_low, mid_grad, start, n1, proj, g1, w, qkv, mixed, lse, sums2, dub):
    rows, feat = xs[0].shape
    seq, d = n1.shape
    hw = mixed.shape[1]
    row = (1, d)
    h = n // 2
    ra = 2 * hw // n
    rb = ra + proj.shape[0] * feat // (nz * n)
    return call(
        functools.partial(attn_bwd_kernel, n, (nz,)), (nz,),
        (idx, *xs, mid_low, mid_grad, start, n1, proj, g1, w, qkv, mixed, lse, sums2, dub),
        [whole((rows, feat))] * nz + [whole((seq, d)), whole((seq, d)), whole((seq, d)), whole((seq, d)),
                                      by_kind((feat, d)), whole(row), part((4 * hw, d)),
                                      part((3 * hw, seq)), part((hw, seq)), part((8, seq)),
                                      whole((4, d)), whole((nz, 1, d))],
        [(piece_out(h, ra, d), sds((h, nz, ra, d), BF16)), (piece_out(h, ra, d), sds((h, nz, ra, d), BF16)),
         (whole((h, nz, rb, d)), sds((h, nz, rb, d), BF16)), (whole((h, nz, rb, d)), sds((h, nz, rb, d), BF16)),
         (whole((nz, rows, feat)), sds((nz, rows, feat), BF16)),
         (whole((8 + 2 * nz, d)), sds((8 + 2 * nz, d), F32))],
        [pltpu.VMEM((seq, d), F32), pltpu.VMEM((3 * hw, seq), BF16), pltpu.VMEM((4 * hw, d), BF16),
         pltpu.VMEM((seq, feat), BF16), pltpu.VMEM((proj.shape[0] * feat, d), BF16),
         pltpu.VMEM((seq, feat), BF16)], work(26))


def place(n, nz, idx, lo, hi, sizes):
    h, rows, d = lo.shape
    col = 256 if d % 256 == 0 else d
    tail = sizes[2:]
    outs = [(n + h, sizes[0]), (h, sizes[1]), (n * nz, tail[0])] if tail else [(n, sizes[0]), (n, sizes[1])]
    spec = lambda a, b: pl.BlockSpec((a, b, col), lambda j, *_: (0, 0, j))
    return call(
        functools.partial(place_kernel, n, sizes, nz), (d // col,), (idx, lo, hi), [spec(h, rows)] * 2,
        [(spec(a, b), sds((a, b, d), F32)) for a, b in outs], [], work(5))


def line_up_kernel(idx, *refs):
    num = len(refs) - 1
    for s, ref in enumerate(refs[:num]):
        refs[num][lax.rem(idx[2] - s + num, num)] = ref[...].astype(refs[num].dtype)


def line_up(nz, idx, blocks, dtype):
    rows, d = blocks[0].shape
    return call(
        line_up_kernel, (1,), (idx, *blocks), [whole((rows, d))] * nz,
        [(whole((nz, rows, d)), sds((nz, rows, d), dtype))], [], work(2))[0]


def per_device(nw, nz, tokens, kind, proj_weight, proj_bias, ln1_gain, ln1_bias, qkv_weight, qv_bias,
               out_weight, out_bias, ln2_gain, ln2_bias, up_weight, up_bias, down_weight, down_bias,
               cotangent):
    d, f = up_weight.shape
    hw = out_weight.shape[0]
    feat = tokens.shape[2]
    n = min(nw, 8)
    me_w = lax.axis_index("wide")
    me_z = lax.axis_index("narrow")
    me = lax.rem(me_w, n)
    my_kind = lax.dynamic_index_in_dim(kind, me_z, 0, keepdims=False)
    idx = jnp.stack([jnp.where(my_kind == 1, 1, 0), me, me_z]).astype(jnp.int32)

    def swap(v, bit):
        return lax.ppermute(v, "wide", [(i, i ^ bit) for i in range(nw)])

    def shift(v, s):
        return lax.ppermute(v, "narrow", [(i, (i + s) % nz) for i in range(nz)])

    def add(a, b):
        return (a.astype(F32) + b.astype(F32)).astype(BF16)

    def to_clip(v):
        return [lax.dynamic_index_in_dim(v, me_z, 0, keepdims=False)] + [
            shift(lax.dynamic_index_in_dim(v, lax.rem(me_z + s, nz), 0, keepdims=False), s)
            for s in range(1, nz)]

    def to_rows(v, dtype):
        return line_up(nz, idx, [v[0]] + [shift(v[s], s) for s in range(1, nz)], dtype)

    def spread(cur, flip, last):
        bufs = [cur]
        for b in step_bits(n, flip)[::-1]:
            now = jnp.concatenate(bufs) if len(bufs) > 1 else bufs[0]
            bufs = [now, swap(now, b)]
        if not last:
            return jnp.concatenate(bufs)
        return bufs + [swap(v, 1) for v in bufs]

    def gather(a, b):
        ra, rb = a.shape[0] // n, b.shape[0] // n
        mine = jnp.concatenate([lax.dynamic_slice_in_dim(a, me * ra, ra, 0),
                                lax.dynamic_slice_in_dim(b, me * rb, rb, 0)])
        got = jnp.stack([shift(mine, s) for s in range(1, nz)])
        return (spread(got[None, :, :ra], False, True),
                spread(got[None, :, ra:], True, True))

    def fold(keep, send, flip):
        got = swap(send, 1)
        for b in step_bits(n, flip):
            h = keep.shape[0] // 2
            go = add(keep[h:], got[h:])
            keep, got = add(keep[:h], got[:h]), swap(go, b)
        total = add(keep[0], got[0])
        for k in range(n.bit_length() - 1, nw.bit_length() - 1):
            total = add(total, swap(total, 1 << k))
        return total

    def over_z(a, b):
        ra = a.shape[1]
        total = [a[0].astype(F32), b[0].astype(F32)]
        for s in range(1, nz):
            both = jnp.concatenate([a[s], b[s]])
            got = shift(both, -s)
            total = [total[0] + got[:ra].astype(F32), total[1] + got[ra:].astype(F32)]
        return total[0].astype(BF16), total[1].astype(BF16)

    def share(a, b, sizes):
        lo = jnp.concatenate([spread(a[None], False, False),
                              spread(b[None], True, False)], axis=1)
        return place(n, nz, idx, lo, swap(lo, 1), sizes)

    xs = to_clip(tokens)
    bias_three = jnp.concatenate([qv_bias[0], jnp.zeros_like(qv_bias[0]), qv_bias[1]])
    bq = jnp.stack([bias_three] + [shift(bias_three, s) for s in range(1, nz)])[:, :, None]
    qkv_t = jnp.transpose(qkv_weight, (1, 2, 0))
    own_a = qkv_t[:2].reshape(2 * hw, d)
    own_b = jnp.concatenate([qkv_t[2], out_weight])
    pa, pb = gather(own_a, own_b)
    fa, fb = gather(up_weight, down_weight)
    gs = to_clip(cotangent)
    r = lambda v: v.reshape(1, d)

    start, n1, qkv, mixed, lse, middle, n2, w = attn_fwd(
        n, nz, idx, xs, proj_weight, proj_bias[:, None, :], r(ln1_gain), r(ln1_bias), own_a, own_b, bq,
        r(out_bias), r(ln2_gain), r(ln2_bias), pa, pb)
    out, mid_grad, mid_low, keep_u, send_u, keep_d, send_d, dub, sums2 = ffn(
        n, nz, idx, gs, n2, middle, up_weight, down_weight, up_bias.reshape(nz, 1, f), r(down_bias),
        r(ln2_gain), fa, fb)
    keep_a, send_a, keep_b, send_b, tok_grad, small = attn_bwd(
        n, nz, idx, xs, mid_low, mid_grad, start, n1, proj_weight, r(ln1_gain), w, qkv, mixed, lse,
        sums2, dub)

    up_z, down_z = over_z(fold(keep_u, send_u, False), fold(keep_d, send_d, True))
    output = to_rows(out, BF16)
    up_g, down_g = share(up_z, down_z, (d // n, f // n))

    tokens_grad = to_rows(tok_grad, F32)
    a_z, b_z = over_z(fold(keep_a, send_a, False), fold(keep_b, send_b, True))
    ra = 2 * hw // n
    tail = b_z[ra:]
    b_all = jnp.concatenate([b_z[:ra], tail] + [shift(tail, s) for s in range(1, nz)])
    a_g, b_g, proj_g = share(a_z, b_all, (ra, ra, tail.shape[0]))

    for k in range(nw.bit_length() - 1):
        small = small + swap(small, 1 << k)
    for k in range(nz.bit_length() - 1):
        small = small + lax.ppermute(small, "narrow", [(i, i ^ (1 << k)) for i in range(nz)])
    up_b = lax.dynamic_index_in_dim(small, 8 + me_z, 0, keepdims=False)
    dqv = lax.dynamic_index_in_dim(small, 8 + nz + me_z, 0, keepdims=False)
    qv = jnp.stack([dqv[:hw], dqv[2 * hw:3 * hw]])
    qkv_g = jnp.transpose(a_g.reshape(3, hw, d), (2, 0, 1))
    return (output, tokens_grad, proj_g.reshape(-1, feat, d), small[0:2], small[2], small[3], qkv_g, qv,
            b_g.reshape(hw, d), small[6], small[4], small[5], up_g.reshape(d, f), up_b, down_g.reshape(f, d),
            small[7])


def solution(mesh):
    in_specs = (
        P("wide", "narrow", None), P("wide"), P(), P(), P(), P(), P(None, None, "narrow"),
        P(None, "narrow"), P("narrow", None), P(), P(), P(), P(None, "narrow"), P(),
        P("narrow", None), P(), P("wide", "narrow", None),
    )
    out_specs = (
        P("wide", "narrow", None), P("wide", "narrow", None), P(), P(), P(), P(),
        P(None, None, "narrow"), P(None, "narrow"), P("narrow", None), P(), P(), P(),
        P(None, "narrow"), P("narrow"), P("narrow", None), P(),
    )
    body = functools.partial(per_device, mesh.shape["wide"], mesh.shape["narrow"])

    return jax.shard_map(body, mesh=mesh, in_specs=in_specs, out_specs=out_specs, check_vma=False)
```

```python
import functools

import jax
import jax.numpy as jnp
from jax import lax
from jax.experimental import pallas as pl
from jax.experimental.pallas import tpu as pltpu
from jax.sharding import PartitionSpec as P


HEAD_DIM = 64
SCALE = HEAD_DIM ** (-0.5)
EPS = 1e-06
F32 = jnp.float32
BF16 = jnp.bfloat16
NN = (((1,), (0,)), ((), ()))
NT = (((1,), (1,)), ((), ()))
TN = (((0,), (0,)), ((), ()))


def dot(a, b, dims):
    return lax.dot_general(a, b, dims, preferred_element_type=F32)


def row_stats(v):
    mean = jnp.mean(v, axis=-1, keepdims=True)
    cen = v - mean
    var = jnp.mean(cen * cen, axis=-1, keepdims=True)
    return cen, lax.rsqrt(var + EPS)


def norm_back(v, grad, gain):
    cen, r = row_stats(v)
    xhat = cen * r
    q = grad * gain
    mq = jnp.mean(q, axis=-1, keepdims=True)
    mqx = jnp.mean(q * xhat, axis=-1, keepdims=True)
    return r * (q - mq - xhat * mqx), xhat


def gelu_pair(u):
    phi = 0.5 * (1.0 + lax.erf(u * (2.0 ** -0.5)))
    dens = jnp.exp(-0.5 * u * u) * 0.3989422804014327
    return u * phi, phi + u * dens


def rows_of(i, size):
    start = i * size
    return pl.ds(pl.multiple_of(start, size & -size), size)


def step_bits(n, flip):
    bits = [1 << k for k in range(1, n.bit_length() - 1)]
    return bits[::-1] if flip else bits


def kept(n, flip):
    order = [0]
    for b in step_bits(n, flip)[::-1]:
        order = order + [r | b for r in order]
    return order


def spread_order(n, flip):
    bits = step_bits(n, flip)[::-1]
    sets = [[0]]
    for b in bits:
        now = [r for one in sets for r in one]
        sets = [now, [r ^ b for r in now]]
    return sets + [[r ^ 1 for r in one] for one in sets]


def put_pieces(dst, base, bufs, me, n, flip):
    for ref, rs in zip(bufs, spread_order(n, flip)):
        size = ref.shape[2]
        for i, r in enumerate(rs):
            dst[rows_of(base // size + (me ^ r), size), :] = ref[i, 0]


def cut_pieces(src, base, keep, send, me, n, flip, size, at=None):
    for i, r in enumerate(kept(n, flip)):
        for ref, q in ((keep, r), (send, r | 1)):
            val = src[rows_of(base // size + (me ^ q), size), :]
            if at is None:
                ref[i, 0] = val
            else:
                ref[i, at, 0:size] = val


def attn_fwd_kernel(n, nbuf, idx, *refs):
    xs, refs = refs[:nbuf[0]], refs[nbuf[0]:]
    proj, pbias, g1, b1, own_a, own_b, bq, ob, g2, b2 = refs[:10]
    refs = refs[10:]
    pa, pb, refs = refs[:nbuf[1]], refs[nbuf[1]:2 * nbuf[1]], refs[2 * nbuf[1]:]
    start, n1, qkv, mixed, lse, middle, n2, w, xfull = refs
    z = pl.program_id(0)
    nz = pl.num_programs(0)
    me = idx[1]
    half = own_a.shape[0]

    @pl.when(z == 0)
    def _():
        part_rows = xs[0].shape[0]
        for s, ref in enumerate(xs):
            xfull[rows_of(lax.rem(idx[2] - s + len(xs), len(xs)), part_rows), :] = ref[...]
        s = dot(xfull[...], proj[0], NN) + pbias[0]
        start[...] = s
        middle[...] = s + ob[...]
        cen, r = row_stats(s)
        n1[...] = (cen * r * g1[...] + b1[...]).astype(BF16)
        w[0, 0:half, :] = own_a[...]
        w[0, half:2 * half, :] = own_b[...]

    @pl.when(z > 0)
    def _():
        put_pieces(w.at[0], 0, pa, me, n, False)
        put_pieces(w.at[0], half, pb, me, n, True)

    width = mixed.shape[1]
    qkv[0] = (dot(w[0, 0:3 * width, :], n1[...], NT) + bq[0]).astype(BF16)
    for h in range(width // HEAD_DIM):
        lo = h * HEAD_DIM
        q_t = qkv[0, lo:lo + HEAD_DIM, :]
        k_t = qkv[0, width + lo:width + lo + HEAD_DIM, :]
        v_t = qkv[0, 2 * width + lo:2 * width + lo + HEAD_DIM, :]
        s = dot(k_t, q_t, TN) * SCALE
        top = jnp.max(s, axis=0, keepdims=True)
        e = jnp.exp(s - top)
        total = jnp.sum(e, axis=0, keepdims=True)
        p = (e * (1.0 / total)).astype(BF16)
        lse[0, h:h + 1, :] = top + jnp.log(total)
        mixed[0, lo:lo + HEAD_DIM, :] = dot(v_t, p, NN).astype(BF16)
    middle[...] += dot(mixed[0], w[0, 3 * width:4 * width, :], TN)

    @pl.when(z == nz - 1)
    def _():
        cen, r = row_stats(middle[...])
        n2[...] = (cen * r * g2[...] + b2[...]).astype(BF16)


def ffn_kernel(n, nbuf, idx, *refs):
    gs, refs = refs[:nbuf[0]], refs[nbuf[0]:]
    n2, middle, own_up, own_down, ub, db, g2 = refs[:7]
    refs = refs[7:]
    pa, pb, refs = refs[:nbuf[1]], refs[nbuf[1]:2 * nbuf[1]], refs[2 * nbuf[1]:]
    out, refs = refs[:nbuf[0]], refs[nbuf[0]:]
    mid_grad, mid_low, keep_u, send_u, keep_d, send_d, dub, sums = refs[:8]
    acc, dn2, n2t, g, up, down, gup, gdown = refs[8:]
    z = pl.program_id(0)
    nz = pl.num_programs(0)
    me = idx[1]
    num = len(gs)

    @pl.when(z == 0)
    def _():
        part_rows = gs[0].shape[0]
        for s, ref in enumerate(gs):
            g[rows_of(lax.rem(idx[2] - s + num, num), part_rows), :] = ref[...]
        acc[...] = middle[...] + db[...]
        dn2[...] = jnp.zeros_like(dn2)
        n2t[...] = n2[...].T
        up[...] = own_up[...]
        down[...] = own_down[...]

    @pl.when(z > 0)
    def _():
        put_pieces(up, 0, pa, me, n, False)
        put_pieces(down, 0, pb, me, n, True)

    u = dot(n2[...], up[...], NN) + ub[0]
    h, slope = gelu_pair(u)
    h = h.astype(BF16)
    acc[...] += dot(h, down[...], NN)
    gdown[...] = dot(h, g[...], TN).astype(BF16)
    pre = (dot(g[...], down[...], NT) * slope).astype(BF16)
    dub[0] = jnp.sum(pre.astype(F32), axis=0, keepdims=True)
    gup[...] = dot(n2t[...], pre, NN).astype(BF16)
    dn2[...] += dot(pre, up[...], NT)
    cut_pieces(gup, 0, keep_u, send_u, me, n, False, gup.shape[0] // n)
    cut_pieces(gdown, 0, keep_d, send_d, me, n, True, gdown.shape[0] // n)

    @pl.when(z == nz - 1)
    def _():
        part_rows = gs[0].shape[0]
        for s in range(num):
            block = rows_of(lax.rem(idx[2] + s, num), part_rows)
            out[s][...] = acc[block, :].astype(BF16)
        gf = g[...].astype(F32)
        d = dn2[...]
        back, xhat = norm_back(middle[...], d, g2[...])
        mg = gf + back
        mid_grad[...] = mg
        ml = mg.astype(BF16)
        mid_low[...] = ml
        sums[...] = jnp.concatenate([
            jnp.sum(d * xhat, axis=0, keepdims=True),
            jnp.sum(d, axis=0, keepdims=True),
            jnp.sum(ml.astype(F32), axis=0, keepdims=True),
            jnp.sum(gf, axis=0, keepdims=True),
        ], axis=0)


def attn_bwd_kernel(n, nbuf, idx, *refs):
    xs, refs = refs[:nbuf[0]], refs[nbuf[0]:]
    mid_low, mid_grad, start, n1, proj, g1, w, qkv, mixed, lse, sums2, dub = refs[:12]
    keep_a, send_a, keep_b, send_b, small = refs[12:17]
    tok_grad, refs = refs[17:17 + nbuf[0]], refs[17 + nbuf[0]:]
    dn1, dqkv, gw, xfull, pair, tok = refs
    z = pl.program_id(0)
    nz = pl.num_programs(0)
    me = idx[1]
    num = len(xs)

    @pl.when(z == 0)
    def _():
        dn1[...] = jnp.zeros_like(dn1)
        small[...] = jnp.zeros_like(small)
        small[4:8, :] = sums2[...]
        for s in range(num):
            small[8 + s:9 + s, :] = dub[s]

    ml = mid_low[...]
    width = mixed.shape[1]
    gw[3 * width:4 * width, :] = dot(mixed[0], ml, NN).astype(BF16)
    do_all = dot(w[0, 3 * width:4 * width, :], ml, NT).astype(BF16)
    for h in range(width // HEAD_DIM):
        lo = h * HEAD_DIM
        q_t = qkv[0, lo:lo + HEAD_DIM, :]
        k_t = qkv[0, width + lo:width + lo + HEAD_DIM, :]
        v_t = qkv[0, 2 * width + lo:2 * width + lo + HEAD_DIM, :]
        do_t = do_all[lo:lo + HEAD_DIM, :]
        p = jnp.exp(dot(k_t, q_t, TN) * SCALE - lse[0, h:h + 1, :])
        dp = dot(v_t, do_t, TN)
        dsum = jnp.sum(p * dp, axis=0, keepdims=True)
        ds = (p * (dp - dsum)).astype(BF16)
        dqkv[lo:lo + HEAD_DIM, :] = (dot(k_t, ds, NN) * SCALE).astype(BF16)
        dqkv[width + lo:width + lo + HEAD_DIM, :] = (dot(q_t, ds, NT) * SCALE).astype(BF16)
        dqkv[2 * width + lo:2 * width + lo + HEAD_DIM, :] = dot(do_t, p.astype(BF16), NT).astype(BF16)
    dw = dqkv[...]
    ones = jnp.ones((8, dw.shape[1]), BF16)
    small[pl.ds(8 + num + lax.rem(idx[2] - z + num, num), 1), 0:3 * width] = dot(ones, dw, NT)[0:1, :]
    gw[0:3 * width, :] = dot(dw, n1[...], NN).astype(BF16)
    dn1[...] += dot(dw, w[0, 0:3 * width, :], TN)
    half = 2 * width
    cut_pieces(gw, 0, keep_a, send_a, me, n, False, half // n)
    cut_pieces(gw, half, keep_b, send_b, me, n, True, half // n, at=z)

    @pl.when(z == nz - 1)
    def _():
        part_rows = xs[0].shape[0]
        for s, ref in enumerate(xs):
            xfull[rows_of(lax.rem(idx[2] - s + num, num), part_rows), :] = ref[...]
        d = dn1[...]
        back, xhat = norm_back(start[...], d, g1[...])
        sl = (mid_grad[...] + back).astype(BF16)
        tok[...] = dot(sl, proj[0], NT).astype(BF16)
        for s in range(num):
            tok_grad[s][...] = tok[rows_of(lax.rem(idx[2] + s, num), part_rows), :]
        feat = proj.shape[1]
        pair[rows_of(idx[0], feat), :] = dot(xfull[...], sl, TN).astype(BF16)
        pair[rows_of(1 - idx[0], feat), :] = jnp.zeros((feat, sl.shape[1]), BF16)
        tail = pair.shape[0] // (num * n)
        for i, r in enumerate(kept(n, True)):
            for s in range(num):
                zz = lax.rem(idx[2] - s + num, num)
                for ref, q in ((keep_b, r), (send_b, r | 1)):
                    ref[i, s, half // n:half // n + tail, :] = pair[rows_of(zz * n + (me ^ q), tail), :]
        small[pl.ds(idx[0], 1), :] = jnp.sum(sl.astype(F32), axis=0, keepdims=True)
        small[2:3, :] = jnp.sum(d * xhat, axis=0, keepdims=True)
        small[3:4, :] = jnp.sum(d, axis=0, keepdims=True)


def place_kernel(n, sizes, nz, idx, lo, hi, a, b, *c):
    me = idx[1]
    ra, rb = sizes[:2]
    h = n // 2
    for src, off in ((lo, 0), (hi, 1)):
        for i, r in enumerate(kept(n, False)):
            a[me ^ (r | off)] = src[i, 0:ra, :].astype(F32)
        for i, r in enumerate(kept(n, True)):
            p = me ^ (r | off)
            val = src[i, ra:ra + rb, :].astype(F32)
            if not c:
                b[p] = val
                continue

            @pl.when(p < h)
            def _():
                a[n + p] = val

            @pl.when(p >= h)
            def _():
                b[p - h] = val

            for s in range(nz):
                first = ra + rb + s * sizes[2]
                zz = lax.rem(idx[2] - s + nz, nz)
                c[0][zz * n + p] = src[i, first:first + sizes[2], :].astype(F32)


def whole(shape):
    return pl.BlockSpec(shape, lambda z, *_: (0,) * len(shape))


def part(shape):
    return pl.BlockSpec((1,) + shape, lambda z, *_: (z,) + (0,) * len(shape))


def true_part(shape, nz):
    return pl.BlockSpec((1,) + shape, lambda z, k: (lax.rem(k[2] - z + nz, nz),) + (0,) * len(shape))


def by_kind(shape):
    return pl.BlockSpec((1,) + shape, lambda z, k: (k[0],) + (0,) * len(shape))


def piece_in(v):
    k, _, r, d = v.shape
    return pl.BlockSpec((k, 1, r, d), lambda z, *_: (0, jnp.maximum(z - 1, 0), 0, 0))


def piece_out(k, r, d):
    return pl.BlockSpec((k, 1, r, d), lambda z, *_: (0, z, 0, 0))


def sds(shape, dtype):
    return jax.ShapeDtypeStruct(shape, dtype)


PARAMS = pltpu.CompilerParams(dimension_semantics=("arbitrary",), vmem_limit_bytes=58 << 20)


def work(us):
    return us * 10 ** 9, us * 10 ** 6, 0


def call(kernel, grid, args, in_specs, outs, scratch, cost=(0, 0, 0)):
    estimate = pl.CostEstimate(flops=cost[0], bytes_accessed=cost[1], transcendentals=cost[2])
    return pl.pallas_call(
        kernel,
        grid_spec=pltpu.PrefetchScalarGridSpec(
            num_scalar_prefetch=1, grid=grid, in_specs=in_specs, out_specs=[s for s, _ in outs],
            scratch_shapes=scratch),
        out_shape=[o for _, o in outs], compiler_params=PARAMS, cost_estimate=estimate,
    )(*args)


def attn_fwd(n, nz, idx, xs, proj, pbias, g1, b1, own_a, own_b, bq, ob, g2, b2, pa, pb):
    rows, feat = xs[0].shape
    half, d = own_a.shape
    hw = half // 2
    seq = rows * nz
    row = (1, d)
    return call(
        functools.partial(attn_fwd_kernel, n, (nz, len(pa))), (nz,),
        (idx, *xs, proj, pbias, g1, b1, own_a, own_b, bq, ob, g2, b2, *pa, *pb),
        [whole((rows, feat))] * nz + [by_kind((feat, d)), by_kind(row), whole(row), whole(row),
                                      whole((half, d)), whole((half, d)), part((3 * hw, 1)),
                                      whole(row), whole(row), whole(row)]
        + [piece_in(v) for v in (*pa, *pb)],
        [(whole((seq, d)), sds((seq, d), F32)), (whole((seq, d)), sds((seq, d), BF16)),
         (part((3 * hw, seq)), sds((nz, 3 * hw, seq), BF16)), (part((hw, seq)), sds((nz, hw, seq), BF16)),
         (part((8, seq)), sds((nz, 8, seq), F32)), (whole((seq, d)), sds((seq, d), F32)),
         (whole((seq, d)), sds((seq, d), BF16)), (part((2 * half, d)), sds((nz, 2 * half, d), BF16))],
        [pltpu.VMEM((seq, feat), BF16)], work(20))


def ffn(n, nz, idx, gs, n2, middle, own_up, own_down, ub, db, g2, pa, pb):
    rows, d = gs[0].shape
    f = own_up.shape[1]
    seq = rows * nz
    row = (1, d)
    h = n // 2
    return call(
        functools.partial(ffn_kernel, n, (nz, len(pa))), (nz,),
        (idx, *gs, n2, middle, own_up, own_down, ub, db, g2, *pa, *pb),
        [whole((rows, d))] * nz + [whole((seq, d)), whole((seq, d)), whole((d, f)), whole((f, d)),
                                   true_part((1, f), nz), whole(row), whole(row)]
        + [piece_in(v) for v in (*pa, *pb)],
        [(whole((rows, d)), sds((rows, d), BF16))] * nz
        + [(whole((seq, d)), sds((seq, d), F32)), (whole((seq, d)), sds((seq, d), BF16)),
         (piece_out(h, d // n, f), sds((h, nz, d // n, f), BF16)),
         (piece_out(h, d // n, f), sds((h, nz, d // n, f), BF16)),
         (piece_out(h, f // n, d), sds((h, nz, f // n, d), BF16)),
         (piece_out(h, f // n, d), sds((h, nz, f // n, d), BF16)),
         (true_part((1, f), nz), sds((nz, 1, f), F32)), (whole((4, d)), sds((4, d), F32))],
        [pltpu.VMEM((seq, d), F32), pltpu.VMEM((seq, d), F32), pltpu.VMEM((d, seq), BF16),
         pltpu.VMEM((seq, d), BF16), pltpu.VMEM((d, f), BF16), pltpu.VMEM((f, d), BF16),
         pltpu.VMEM((d, f), BF16), pltpu.VMEM((f, d), BF16)], work(26))


def attn_bwd(n, nz, idx, xs, mid_low, mid_grad, start, n1, proj, g1, w, qkv, mixed, lse, sums2, dub):
    rows, feat = xs[0].shape
    seq, d = n1.shape
    hw = mixed.shape[1]
    row = (1, d)
    h = n // 2
    ra = 2 * hw // n
    rb = ra + proj.shape[0] * feat // (nz * n)
    return call(
        functools.partial(attn_bwd_kernel, n, (nz,)), (nz,),
        (idx, *xs, mid_low, mid_grad, start, n1, proj, g1, w, qkv, mixed, lse, sums2, dub),
        [whole((rows, feat))] * nz + [whole((seq, d)), whole((seq, d)), whole((seq, d)), whole((seq, d)),
                                      by_kind((feat, d)), whole(row), part((4 * hw, d)),
                                      part((3 * hw, seq)), part((hw, seq)), part((8, seq)),
                                      whole((4, d)), whole((nz, 1, d))],
        [(piece_out(h, ra, d), sds((h, nz, ra, d), BF16)), (piece_out(h, ra, d), sds((h, nz, ra, d), BF16)),
         (whole((h, nz, rb, d)), sds((h, nz, rb, d), BF16)), (whole((h, nz, rb, d)), sds((h, nz, rb, d), BF16)),
         (whole((8 + 2 * nz, d)), sds((8 + 2 * nz, d), F32))]
        + [(whole((rows, feat)), sds((rows, feat), BF16))] * nz,
        [pltpu.VMEM((seq, d), F32), pltpu.VMEM((3 * hw, seq), BF16), pltpu.VMEM((4 * hw, d), BF16),
         pltpu.VMEM((seq, feat), BF16), pltpu.VMEM((proj.shape[0] * feat, d), BF16),
         pltpu.VMEM((seq, feat), BF16)], work(26))


def place(n, nz, idx, lo, hi, sizes):
    h, rows, d = lo.shape
    col = 256 if d % 256 == 0 else d
    tail = sizes[2:]
    outs = [(n + h, sizes[0]), (h, sizes[1]), (n * nz, tail[0])] if tail else [(n, sizes[0]), (n, sizes[1])]
    spec = lambda a, b: pl.BlockSpec((a, b, col), lambda j, *_: (0, 0, j))
    return call(
        functools.partial(place_kernel, n, sizes, nz), (d // col,), (idx, lo, hi), [spec(h, rows)] * 2,
        [(spec(a, b), sds((a, b, d), F32)) for a, b in outs], [], work(5))


def line_up_kernel(idx, *refs):
    num = len(refs) - 1
    for s, ref in enumerate(refs[:num]):
        refs[num][lax.rem(idx[2] - s + num, num)] = ref[...].astype(refs[num].dtype)


def line_up(nz, idx, blocks, dtype):
    rows, d = blocks[0].shape
    return call(
        line_up_kernel, (1,), (idx, *blocks), [whole((rows, d))] * nz,
        [(whole((nz, rows, d)), sds((nz, rows, d), dtype))], [], work(2))[0]


def per_device(nw, nz, tokens, kind, proj_weight, proj_bias, ln1_gain, ln1_bias, qkv_weight, qv_bias,
               out_weight, out_bias, ln2_gain, ln2_bias, up_weight, up_bias, down_weight, down_bias,
               cotangent):
    d, f = up_weight.shape
    hw = out_weight.shape[0]
    feat = tokens.shape[2]
    n = min(nw, 8)
    me_w = lax.axis_index("wide")
    me_z = lax.axis_index("narrow")
    me = lax.rem(me_w, n)
    my_kind = lax.dynamic_index_in_dim(kind, me_z, 0, keepdims=False)
    idx = jnp.stack([jnp.where(my_kind == 1, 1, 0), me, me_z]).astype(jnp.int32)

    def swap(v, bit):
        return lax.ppermute(v, "wide", [(i, i ^ bit) for i in range(nw)])

    def shift(v, s):
        return lax.ppermute(v, "narrow", [(i, (i + s) % nz) for i in range(nz)])

    def add(a, b):
        return (a.astype(F32) + b.astype(F32)).astype(BF16)

    def to_clip(v):
        return [lax.dynamic_index_in_dim(v, me_z, 0, keepdims=False)] + [
            shift(lax.dynamic_index_in_dim(v, lax.rem(me_z + s, nz), 0, keepdims=False), s)
            for s in range(1, nz)]

    def to_rows(v, dtype):
        return line_up(nz, idx, [v[0]] + [shift(v[s], s) for s in range(1, nz)], dtype)

    def spread(cur, flip, last):
        bufs = [cur]
        for b in step_bits(n, flip)[::-1]:
            now = jnp.concatenate(bufs) if len(bufs) > 1 else bufs[0]
            bufs = [now, swap(now, b)]
        if not last:
            return jnp.concatenate(bufs)
        return bufs + [swap(v, 1) for v in bufs]

    def gather(a, b):
        ra, rb = a.shape[0] // n, b.shape[0] // n
        mine = jnp.concatenate([lax.dynamic_slice_in_dim(a, me * ra, ra, 0),
                                lax.dynamic_slice_in_dim(b, me * rb, rb, 0)])
        got = jnp.stack([shift(mine, s) for s in range(1, nz)])
        return (spread(got[None, :, :ra], False, True),
                spread(got[None, :, ra:], True, True))

    def fold(keep, send, flip):
        got = swap(send, 1)
        for b in step_bits(n, flip):
            h = keep.shape[0] // 2
            go = add(keep[h:], got[h:])
            keep, got = add(keep[:h], got[:h]), swap(go, b)
        total = add(keep[0], got[0])
        for k in range(n.bit_length() - 1, nw.bit_length() - 1):
            total = add(total, swap(total, 1 << k))
        return total

    def over_z(a, b):
        ra = a.shape[1]
        total = [a[0].astype(F32), b[0].astype(F32)]
        for s in range(1, nz):
            both = jnp.concatenate([a[s], b[s]])
            got = shift(both, -s)
            total = [total[0] + got[:ra].astype(F32), total[1] + got[ra:].astype(F32)]
        return total[0].astype(BF16), total[1].astype(BF16)

    def share(a, b, sizes):
        lo = jnp.concatenate([spread(a[None], False, False),
                              spread(b[None], True, False)], axis=1)
        return place(n, nz, idx, lo, swap(lo, 1), sizes)

    xs = to_clip(tokens)
    bias_three = jnp.concatenate([qv_bias[0], jnp.zeros_like(qv_bias[0]), qv_bias[1]])
    bq = jnp.stack([bias_three] + [shift(bias_three, s) for s in range(1, nz)])[:, :, None]
    qkv_t = jnp.transpose(qkv_weight, (1, 2, 0))
    own_a = qkv_t[:2].reshape(2 * hw, d)
    own_b = jnp.concatenate([qkv_t[2], out_weight])
    pa, pb = gather(own_a, own_b)
    fa, fb = gather(up_weight, down_weight)
    gs = to_clip(cotangent)
    r = lambda v: v.reshape(1, d)

    start, n1, qkv, mixed, lse, middle, n2, w = attn_fwd(
        n, nz, idx, xs, proj_weight, proj_bias[:, None, :], r(ln1_gain), r(ln1_bias), own_a, own_b, bq,
        r(out_bias), r(ln2_gain), r(ln2_bias), pa, pb)
    *out, mid_grad, mid_low, keep_u, send_u, keep_d, send_d, dub, sums2 = ffn(
        n, nz, idx, gs, n2, middle, up_weight, down_weight, up_bias.reshape(nz, 1, f), r(down_bias),
        r(ln2_gain), fa, fb)
    keep_a, send_a, keep_b, send_b, small, *tok_grad = attn_bwd(
        n, nz, idx, xs, mid_low, mid_grad, start, n1, proj_weight, r(ln1_gain), w, qkv, mixed, lse,
        sums2, dub)

    up_z, down_z = over_z(fold(keep_u, send_u, False), fold(keep_d, send_d, True))
    output = to_rows(out, BF16)
    up_g, down_g = share(up_z, down_z, (d // n, f // n))

    tokens_grad = to_rows(tok_grad, F32)
    a_z, b_z = over_z(fold(keep_a, send_a, False), fold(keep_b, send_b, True))
    ra = 2 * hw // n
    tail = b_z[ra:]
    b_all = jnp.concatenate([b_z[:ra], tail] + [shift(tail, s) for s in range(1, nz)])
    a_g, b_g, proj_g = share(a_z, b_all, (ra, ra, tail.shape[0]))

    for k in range(nw.bit_length() - 1):
        small = small + swap(small, 1 << k)
    for k in range(nz.bit_length() - 1):
        small = small + lax.ppermute(small, "narrow", [(i, i ^ (1 << k)) for i in range(nz)])
    up_b = lax.dynamic_index_in_dim(small, 8 + me_z, 0, keepdims=False)
    dqv = lax.dynamic_index_in_dim(small, 8 + nz + me_z, 0, keepdims=False)
    qv = jnp.stack([dqv[:hw], dqv[2 * hw:3 * hw]])
    qkv_g = jnp.transpose(a_g.reshape(3, hw, d), (2, 0, 1))
    return (output, tokens_grad, proj_g.reshape(-1, feat, d), small[0:2], small[2], small[3], qkv_g, qv,
            b_g.reshape(hw, d), small[6], small[4], small[5], up_g.reshape(d, f), up_b, down_g.reshape(f, d),
            small[7])


def solution(mesh):
    in_specs = (
        P("wide", "narrow", None), P("wide"), P(), P(), P(), P(), P(None, None, "narrow"),
        P(None, "narrow"), P("narrow", None), P(), P(), P(), P(None, "narrow"), P(),
        P("narrow", None), P(), P("wide", "narrow", None),
    )
    out_specs = (
        P("wide", "narrow", None), P("wide", "narrow", None), P(), P(), P(), P(),
        P(None, None, "narrow"), P(None, "narrow"), P("narrow", None), P(), P(), P(),
        P(None, "narrow"), P("narrow"), P("narrow", None), P(),
    )
    body = functools.partial(per_device, mesh.shape["wide"], mesh.shape["narrow"])

    return jax.shard_map(body, mesh=mesh, in_specs=in_specs, out_specs=out_specs, check_vma=False)
```

```python
import functools

import jax
import jax.numpy as jnp
from jax import lax
from jax.experimental import pallas as pl
from jax.experimental.pallas import tpu as pltpu
from jax.sharding import PartitionSpec as P


HEAD_DIM = 64
SCALE = HEAD_DIM ** (-0.5)
EPS = 1e-06
F32 = jnp.float32
BF16 = jnp.bfloat16
NN = (((1,), (0,)), ((), ()))
NT = (((1,), (1,)), ((), ()))
TN = (((0,), (0,)), ((), ()))


def dot(a, b, dims):
    return lax.dot_general(a, b, dims, preferred_element_type=F32)


def row_stats(v):
    mean = jnp.mean(v, axis=-1, keepdims=True)
    cen = v - mean
    var = jnp.mean(cen * cen, axis=-1, keepdims=True)
    return cen, lax.rsqrt(var + EPS)


def norm_back(v, grad, gain):
    cen, r = row_stats(v)
    xhat = cen * r
    q = grad * gain
    mq = jnp.mean(q, axis=-1, keepdims=True)
    mqx = jnp.mean(q * xhat, axis=-1, keepdims=True)
    return r * (q - mq - xhat * mqx), xhat


def gelu_pair(u):
    phi = 0.5 * (1.0 + lax.erf(u * (2.0 ** -0.5)))
    dens = jnp.exp(-0.5 * u * u) * 0.3989422804014327
    return u * phi, phi + u * dens


def rows_of(i, size):
    start = i * size
    return pl.ds(pl.multiple_of(start, size & -size), size)


def step_bits(n, flip):
    bits = [1 << k for k in range(1, n.bit_length() - 1)]
    return bits[::-1] if flip else bits


def kept(n, flip):
    order = [0]
    for b in step_bits(n, flip)[::-1]:
        order = order + [r | b for r in order]
    return order


def spread_order(n, flip):
    bits = step_bits(n, flip)[::-1]
    sets = [[0]]
    for b in bits:
        now = [r for one in sets for r in one]
        sets = [now, [r ^ b for r in now]]
    return sets + [[r ^ 1 for r in one] for one in sets]


def put_pieces(dst, base, bufs, me, n, flip):
    for ref, rs in zip(bufs, spread_order(n, flip)):
        size = ref.shape[2]
        for i, r in enumerate(rs):
            dst[rows_of(base // size + (me ^ r), size), :] = ref[i, 0]


def cut_pieces(src, base, keep, send, me, n, flip, size, at=None):
    for i, r in enumerate(kept(n, flip)):
        for ref, q in ((keep, r), (send, r | 1)):
            val = src[rows_of(base // size + (me ^ q), size), :]
            if at is None:
                ref[i, 0] = val
            else:
                ref[i, at, 0:size] = val


def attn_fwd_kernel(n, nbuf, idx, *refs):
    xs, refs = refs[:nbuf[0]], refs[nbuf[0]:]
    proj, vec, own_a, own_b, bq = refs[:5]
    refs = refs[5:]
    pa, pb, refs = refs[:nbuf[1]], refs[nbuf[1]:2 * nbuf[1]], refs[2 * nbuf[1]:]
    start, n1, qkv, mixed, lse, middle, n2, w, xfull = refs
    z = pl.program_id(0)
    nz = pl.num_programs(0)
    me = idx[1]
    half = own_a.shape[0]

    @pl.when(z == 0)
    def _():
        part_rows = xs[0].shape[0]
        for s, ref in enumerate(xs):
            xfull[rows_of(lax.rem(idx[2] - s + len(xs), len(xs)), part_rows), :] = ref[...]
        s = dot(xfull[...], proj[0], NN) + vec[pl.ds(6 + idx[0], 1), :]
        start[...] = s
        middle[...] = s + vec[2:3, :]
        cen, r = row_stats(s)
        n1[...] = (cen * r * vec[0:1, :] + vec[1:2, :]).astype(BF16)
        w[0, 0:half, :] = own_a[...]
        w[0, half:2 * half, :] = own_b[...]

    @pl.when(z > 0)
    def _():
        put_pieces(w.at[0], 0, pa, me, n, False)
        put_pieces(w.at[0], half, pb, me, n, True)

    width = mixed.shape[1]
    qkv[0] = (dot(w[0, 0:3 * width, :], n1[...], NT) + bq[0]).astype(BF16)
    for h in range(width // HEAD_DIM):
        lo = h * HEAD_DIM
        q_t = qkv[0, lo:lo + HEAD_DIM, :]
        k_t = qkv[0, width + lo:width + lo + HEAD_DIM, :]
        v_t = qkv[0, 2 * width + lo:2 * width + lo + HEAD_DIM, :]
        s = dot(k_t, q_t, TN) * SCALE
        top = jnp.max(s, axis=0, keepdims=True)
        e = jnp.exp(s - top)
        total = jnp.sum(e, axis=0, keepdims=True)
        p = (e * (1.0 / total)).astype(BF16)
        lse[0, h:h + 1, :] = top + jnp.log(total)
        mixed[0, lo:lo + HEAD_DIM, :] = dot(v_t, p, NN).astype(BF16)
    middle[...] += dot(mixed[0], w[0, 3 * width:4 * width, :], TN)

    @pl.when(z == nz - 1)
    def _():
        cen, r = row_stats(middle[...])
        n2[...] = (cen * r * vec[3:4, :] + vec[4:5, :]).astype(BF16)


def ffn_kernel(n, nbuf, idx, *refs):
    gs, refs = refs[:nbuf[0]], refs[nbuf[0]:]
    n2, middle, own_up, own_down, ub, vec = refs[:6]
    refs = refs[6:]
    pa, pb, refs = refs[:nbuf[1]], refs[nbuf[1]:2 * nbuf[1]], refs[2 * nbuf[1]:]
    out, refs = refs[:nbuf[0]], refs[nbuf[0]:]
    mid_grad, mid_low, keep_u, send_u, keep_d, send_d, dub, sums = refs[:8]
    acc, dn2, n2t, g, up, down, gup, gdown = refs[8:]
    z = pl.program_id(0)
    nz = pl.num_programs(0)
    me = idx[1]
    num = len(gs)

    @pl.when(z == 0)
    def _():
        part_rows = gs[0].shape[0]
        for s, ref in enumerate(gs):
            g[rows_of(lax.rem(idx[2] - s + num, num), part_rows), :] = ref[...]
        acc[...] = middle[...] + vec[5:6, :]
        dn2[...] = jnp.zeros_like(dn2)
        n2t[...] = n2[...].T
        up[...] = own_up[...]
        down[...] = own_down[...]

    @pl.when(z > 0)
    def _():
        put_pieces(up, 0, pa, me, n, False)
        put_pieces(down, 0, pb, me, n, True)

    u = dot(n2[...], up[...], NN) + ub[0]
    h, slope = gelu_pair(u)
    h = h.astype(BF16)
    acc[...] += dot(h, down[...], NN)
    gdown[...] = dot(h, g[...], TN).astype(BF16)
    pre = (dot(g[...], down[...], NT) * slope).astype(BF16)
    dub[0] = jnp.sum(pre.astype(F32), axis=0, keepdims=True)
    gup[...] = dot(n2t[...], pre, NN).astype(BF16)
    dn2[...] += dot(pre, up[...], NT)
    cut_pieces(gup, 0, keep_u, send_u, me, n, False, gup.shape[0] // n)
    cut_pieces(gdown, 0, keep_d, send_d, me, n, True, gdown.shape[0] // n)

    @pl.when(z == nz - 1)
    def _():
        part_rows = gs[0].shape[0]
        for s in range(num):
            block = rows_of(lax.rem(idx[2] + s, num), part_rows)
            out[s][...] = acc[block, :].astype(BF16)
        gf = g[...].astype(F32)
        d = dn2[...]
        back, xhat = norm_back(middle[...], d, vec[3:4, :])
        mg = gf + back
        mid_grad[...] = mg
        ml = mg.astype(BF16)
        mid_low[...] = ml
        sums[...] = jnp.concatenate([
            jnp.sum(d * xhat, axis=0, keepdims=True),
            jnp.sum(d, axis=0, keepdims=True),
            jnp.sum(ml.astype(F32), axis=0, keepdims=True),
            jnp.sum(gf, axis=0, keepdims=True),
        ], axis=0)


def attn_bwd_kernel(n, nbuf, idx, *refs):
    xs, refs = refs[:nbuf[0]], refs[nbuf[0]:]
    mid_low, mid_grad, start, n1, proj, vec, w, qkv, mixed, lse, sums2, dub = refs[:12]
    keep_a, send_a, keep_b, send_b, small = refs[12:17]
    tok_grad, refs = refs[17:17 + nbuf[0]], refs[17 + nbuf[0]:]
    dn1, dqkv, gw, xfull, pair, tok = refs
    z = pl.program_id(0)
    nz = pl.num_programs(0)
    me = idx[1]
    num = len(xs)

    @pl.when(z == 0)
    def _():
        dn1[...] = jnp.zeros_like(dn1)
        small[...] = jnp.zeros_like(small)
        small[4:8, :] = sums2[...]
        for s in range(num):
            small[8 + s:9 + s, :] = dub[s]

    ml = mid_low[...]
    width = mixed.shape[1]
    gw[3 * width:4 * width, :] = dot(mixed[0], ml, NN).astype(BF16)
    do_all = dot(w[0, 3 * width:4 * width, :], ml, NT).astype(BF16)
    for h in range(width // HEAD_DIM):
        lo = h * HEAD_DIM
        q_t = qkv[0, lo:lo + HEAD_DIM, :]
        k_t = qkv[0, width + lo:width + lo + HEAD_DIM, :]
        v_t = qkv[0, 2 * width + lo:2 * width + lo + HEAD_DIM, :]
        do_t = do_all[lo:lo + HEAD_DIM, :]
        p = jnp.exp(dot(k_t, q_t, TN) * SCALE - lse[0, h:h + 1, :])
        dp = dot(v_t, do_t, TN)
        dsum = jnp.sum(p * dp, axis=0, keepdims=True)
        ds = (p * (dp - dsum)).astype(BF16)
        dqkv[lo:lo + HEAD_DIM, :] = (dot(k_t, ds, NN) * SCALE).astype(BF16)
        dqkv[width + lo:width + lo + HEAD_DIM, :] = (dot(q_t, ds, NT) * SCALE).astype(BF16)
        dqkv[2 * width + lo:2 * width + lo + HEAD_DIM, :] = dot(do_t, p.astype(BF16), NT).astype(BF16)
    dw = dqkv[...]
    ones = jnp.ones((8, dw.shape[1]), BF16)
    small[pl.ds(8 + num + lax.rem(idx[2] - z + num, num), 1), 0:3 * width] = dot(ones, dw, NT)[0:1, :]
    gw[0:3 * width, :] = dot(dw, n1[...], NN).astype(BF16)
    dn1[...] += dot(dw, w[0, 0:3 * width, :], TN)
    half = 2 * width
    cut_pieces(gw, 0, keep_a, send_a, me, n, False, half // n)
    cut_pieces(gw, half, keep_b, send_b, me, n, True, half // n, at=z)

    @pl.when(z == nz - 1)
    def _():
        part_rows = xs[0].shape[0]
        for s, ref in enumerate(xs):
            xfull[rows_of(lax.rem(idx[2] - s + num, num), part_rows), :] = ref[...]
        d = dn1[...]
        back, xhat = norm_back(start[...], d, vec[0:1, :])
        sl = (mid_grad[...] + back).astype(BF16)
        tok[...] = dot(sl, proj[0], NT).astype(BF16)
        for s in range(num):
            tok_grad[s][...] = tok[rows_of(lax.rem(idx[2] + s, num), part_rows), :]
        feat = proj.shape[1]
        pair[rows_of(idx[0], feat), :] = dot(xfull[...], sl, TN).astype(BF16)
        pair[rows_of(1 - idx[0], feat), :] = jnp.zeros((feat, sl.shape[1]), BF16)
        tail = pair.shape[0] // (num * n)
        for i, r in enumerate(kept(n, True)):
            for s in range(num):
                zz = lax.rem(idx[2] - s + num, num)
                for ref, q in ((keep_b, r), (send_b, r | 1)):
                    ref[i, s, half // n:half // n + tail, :] = pair[rows_of(zz * n + (me ^ q), tail), :]
        small[pl.ds(idx[0], 1), :] = jnp.sum(sl.astype(F32), axis=0, keepdims=True)
        small[2:3, :] = jnp.sum(d * xhat, axis=0, keepdims=True)
        small[3:4, :] = jnp.sum(d, axis=0, keepdims=True)


def place_kernel(n, sizes, nz, idx, lo, hi, a, b, *c):
    me = idx[1]
    ra, rb = sizes[:2]
    h = n // 2
    for src, off in ((lo, 0), (hi, 1)):
        for i, r in enumerate(kept(n, False)):
            a[me ^ (r | off)] = src[i, 0:ra, :].astype(F32)
        for i, r in enumerate(kept(n, True)):
            p = me ^ (r | off)
            val = src[i, ra:ra + rb, :].astype(F32)
            if not c:
                b[p] = val
                continue

            @pl.when(p < h)
            def _():
                a[n + p] = val

            @pl.when(p >= h)
            def _():
                b[p - h] = val

            for s in range(nz):
                first = ra + rb + s * sizes[2]
                zz = lax.rem(idx[2] - s + nz, nz)
                c[0][zz * n + p] = src[i, first:first + sizes[2], :].astype(F32)


def whole(shape):
    return pl.BlockSpec(shape, lambda z, *_: (0,) * len(shape))


def part(shape):
    return pl.BlockSpec((1,) + shape, lambda z, *_: (z,) + (0,) * len(shape))


def true_part(shape, nz):
    return pl.BlockSpec((1,) + shape, lambda z, k: (lax.rem(k[2] - z + nz, nz),) + (0,) * len(shape))


def by_kind(shape):
    return pl.BlockSpec((1,) + shape, lambda z, k: (k[0],) + (0,) * len(shape))


def piece_in(v):
    k, _, r, d = v.shape
    return pl.BlockSpec((k, 1, r, d), lambda z, *_: (0, jnp.maximum(z - 1, 0), 0, 0))


def piece_out(k, r, d):
    return pl.BlockSpec((k, 1, r, d), lambda z, *_: (0, z, 0, 0))


def sds(shape, dtype):
    return jax.ShapeDtypeStruct(shape, dtype)


PARAMS = pltpu.CompilerParams(dimension_semantics=("arbitrary",), vmem_limit_bytes=58 << 20)


def work(us):
    return us * 10 ** 9, us * 10 ** 6, 0


def call(kernel, grid, args, in_specs, outs, scratch, cost=(0, 0, 0)):
    estimate = pl.CostEstimate(flops=cost[0], bytes_accessed=cost[1], transcendentals=cost[2])
    return pl.pallas_call(
        kernel,
        grid_spec=pltpu.PrefetchScalarGridSpec(
            num_scalar_prefetch=1, grid=grid, in_specs=in_specs, out_specs=[s for s, _ in outs],
            scratch_shapes=scratch),
        out_shape=[o for _, o in outs], compiler_params=PARAMS, cost_estimate=estimate,
    )(*args)


def attn_fwd(n, nz, idx, xs, proj, vec, own_a, own_b, bq, pa, pb):
    rows, feat = xs[0].shape
    half, d = own_a.shape
    hw = half // 2
    seq = rows * nz
    return call(
        functools.partial(attn_fwd_kernel, n, (nz, len(pa))), (nz,),
        (idx, *xs, proj, vec, own_a, own_b, bq, *pa, *pb),
        [whole((rows, feat))] * nz + [by_kind((feat, d)), whole(vec.shape), whole((half, d)),
                                      whole((half, d)), part((3 * hw, 1))]
        + [piece_in(v) for v in (*pa, *pb)],
        [(whole((seq, d)), sds((seq, d), F32)), (whole((seq, d)), sds((seq, d), BF16)),
         (part((3 * hw, seq)), sds((nz, 3 * hw, seq), BF16)), (part((hw, seq)), sds((nz, hw, seq), BF16)),
         (part((8, seq)), sds((nz, 8, seq), F32)), (whole((seq, d)), sds((seq, d), F32)),
         (whole((seq, d)), sds((seq, d), BF16)), (part((2 * half, d)), sds((nz, 2 * half, d), BF16))],
        [pltpu.VMEM((seq, feat), BF16)], work(20))


def ffn(n, nz, idx, gs, n2, middle, own_up, own_down, ub, vec, pa, pb):
    rows, d = gs[0].shape
    f = own_up.shape[1]
    seq = rows * nz
    h = n // 2
    return call(
        functools.partial(ffn_kernel, n, (nz, len(pa))), (nz,),
        (idx, *gs, n2, middle, own_up, own_down, ub, vec, *pa, *pb),
        [whole((rows, d))] * nz + [whole((seq, d)), whole((seq, d)), whole((d, f)), whole((f, d)),
                                   true_part((1, f), nz), whole(vec.shape)]
        + [piece_in(v) for v in (*pa, *pb)],
        [(whole((rows, d)), sds((rows, d), BF16))] * nz
        + [(whole((seq, d)), sds((seq, d), F32)), (whole((seq, d)), sds((seq, d), BF16)),
         (piece_out(h, d // n, f), sds((h, nz, d // n, f), BF16)),
         (piece_out(h, d // n, f), sds((h, nz, d // n, f), BF16)),
         (piece_out(h, f // n, d), sds((h, nz, f // n, d), BF16)),
         (piece_out(h, f // n, d), sds((h, nz, f // n, d), BF16)),
         (true_part((1, f), nz), sds((nz, 1, f), F32)), (whole((4, d)), sds((4, d), F32))],
        [pltpu.VMEM((seq, d), F32), pltpu.VMEM((seq, d), F32), pltpu.VMEM((d, seq), BF16),
         pltpu.VMEM((seq, d), BF16), pltpu.VMEM((d, f), BF16), pltpu.VMEM((f, d), BF16),
         pltpu.VMEM((d, f), BF16), pltpu.VMEM((f, d), BF16)], work(26))


def attn_bwd(n, nz, idx, xs, mid_low, mid_grad, start, n1, proj, vec, w, qkv, mixed, lse, sums2, dub):
    rows, feat = xs[0].shape
    seq, d = n1.shape
    hw = mixed.shape[1]
    h = n // 2
    ra = 2 * hw // n
    rb = ra + proj.shape[0] * feat // (nz * n)
    return call(
        functools.partial(attn_bwd_kernel, n, (nz,)), (nz,),
        (idx, *xs, mid_low, mid_grad, start, n1, proj, vec, w, qkv, mixed, lse, sums2, dub),
        [whole((rows, feat))] * nz + [whole((seq, d)), whole((seq, d)), whole((seq, d)), whole((seq, d)),
                                      by_kind((feat, d)), whole(vec.shape), part((4 * hw, d)),
                                      part((3 * hw, seq)), part((hw, seq)), part((8, seq)),
                                      whole((4, d)), whole((nz, 1, d))],
        [(piece_out(h, ra, d), sds((h, nz, ra, d), BF16)), (piece_out(h, ra, d), sds((h, nz, ra, d), BF16)),
         (whole((h, nz, rb, d)), sds((h, nz, rb, d), BF16)), (whole((h, nz, rb, d)), sds((h, nz, rb, d), BF16)),
         (whole((8 + 2 * nz, d)), sds((8 + 2 * nz, d), F32))]
        + [(whole((rows, feat)), sds((rows, feat), BF16))] * nz,
        [pltpu.VMEM((seq, d), F32), pltpu.VMEM((3 * hw, seq), BF16), pltpu.VMEM((4 * hw, d), BF16),
         pltpu.VMEM((seq, feat), BF16), pltpu.VMEM((proj.shape[0] * feat, d), BF16),
         pltpu.VMEM((seq, feat), BF16)], work(26))


def place(n, nz, idx, lo, hi, sizes):
    h, rows, d = lo.shape
    col = 256 if d % 256 == 0 else d
    tail = sizes[2:]
    outs = [(n + h, sizes[0]), (h, sizes[1]), (n * nz, tail[0])] if tail else [(n, sizes[0]), (n, sizes[1])]
    spec = lambda a, b: pl.BlockSpec((a, b, col), lambda j, *_: (0, 0, j))
    return call(
        functools.partial(place_kernel, n, sizes, nz), (d // col,), (idx, lo, hi), [spec(h, rows)] * 2,
        [(spec(a, b), sds((a, b, d), F32)) for a, b in outs], [], work(5))


def line_up_kernel(idx, *refs):
    num = len(refs) - 1
    for s, ref in enumerate(refs[:num]):
        refs[num][lax.rem(idx[2] - s + num, num)] = ref[...].astype(refs[num].dtype)


def line_up(nz, idx, blocks, dtype):
    rows, d = blocks[0].shape
    return call(
        line_up_kernel, (1,), (idx, *blocks), [whole((rows, d))] * nz,
        [(whole((nz, rows, d)), sds((nz, rows, d), dtype))], [], work(2))[0]


def per_device(nw, nz, tokens, kind, proj_weight, proj_bias, ln1_gain, ln1_bias, qkv_weight, qv_bias,
               out_weight, out_bias, ln2_gain, ln2_bias, up_weight, up_bias, down_weight, down_bias,
               cotangent):
    d, f = up_weight.shape
    hw = out_weight.shape[0]
    feat = tokens.shape[2]
    n = min(nw, 8)
    me_w = lax.axis_index("wide")
    me_z = lax.axis_index("narrow")
    me = lax.rem(me_w, n)
    my_kind = lax.dynamic_index_in_dim(kind, me_z, 0, keepdims=False)
    idx = jnp.stack([jnp.where(my_kind == 1, 1, 0), me, me_z]).astype(jnp.int32)

    def swap(v, bit):
        return lax.ppermute(v, "wide", [(i, i ^ bit) for i in range(nw)])

    def shift(v, s):
        return lax.ppermute(v, "narrow", [(i, (i + s) % nz) for i in range(nz)])

    def add(a, b):
        return (a.astype(F32) + b.astype(F32)).astype(BF16)

    def to_clip(v):
        return [lax.dynamic_index_in_dim(v, me_z, 0, keepdims=False)] + [
            shift(lax.dynamic_index_in_dim(v, lax.rem(me_z + s, nz), 0, keepdims=False), s)
            for s in range(1, nz)]

    def to_rows(v, dtype):
        return line_up(nz, idx, [v[0]] + [shift(v[s], s) for s in range(1, nz)], dtype)

    def spread(cur, flip, last):
        bufs = [cur]
        for b in step_bits(n, flip)[::-1]:
            now = jnp.concatenate(bufs) if len(bufs) > 1 else bufs[0]
            bufs = [now, swap(now, b)]
        if not last:
            return jnp.concatenate(bufs)
        return bufs + [swap(v, 1) for v in bufs]

    def gather(a, b):
        ra, rb = a.shape[0] // n, b.shape[0] // n
        mine = jnp.concatenate([lax.dynamic_slice_in_dim(a, me * ra, ra, 0),
                                lax.dynamic_slice_in_dim(b, me * rb, rb, 0)])
        got = jnp.stack([shift(mine, s) for s in range(1, nz)])
        return (spread(got[None, :, :ra], False, True),
                spread(got[None, :, ra:], True, True))

    def fold(keep, send, flip):
        got = swap(send, 1)
        for b in step_bits(n, flip):
            h = keep.shape[0] // 2
            go = add(keep[h:], got[h:])
            keep, got = add(keep[:h], got[:h]), swap(go, b)
        total = add(keep[0], got[0])
        for k in range(n.bit_length() - 1, nw.bit_length() - 1):
            total = add(total, swap(total, 1 << k))
        return total

    def over_z(a, b):
        ra = a.shape[1]
        total = [a[0].astype(F32), b[0].astype(F32)]
        for s in range(1, nz):
            both = jnp.concatenate([a[s], b[s]])
            got = shift(both, -s)
            total = [total[0] + got[:ra].astype(F32), total[1] + got[ra:].astype(F32)]
        return total[0].astype(BF16), total[1].astype(BF16)

    def share(a, b, sizes):
        lo = jnp.concatenate([spread(a[None], False, False),
                              spread(b[None], True, False)], axis=1)
        return place(n, nz, idx, lo, swap(lo, 1), sizes)

    xs = to_clip(tokens)
    bias_three = jnp.concatenate([qv_bias[0], jnp.zeros_like(qv_bias[0]), qv_bias[1]])
    bq = jnp.stack([bias_three] + [shift(bias_three, s) for s in range(1, nz)])[:, :, None]
    qkv_t = jnp.transpose(qkv_weight, (1, 2, 0))
    own_a = qkv_t[:2].reshape(2 * hw, d)
    own_b = jnp.concatenate([qkv_t[2], out_weight])
    pa, pb = gather(own_a, own_b)
    fa, fb = gather(up_weight, down_weight)
    gs = to_clip(cotangent)
    vec = jnp.concatenate([
        jnp.stack([ln1_gain, ln1_bias, out_bias, ln2_gain, ln2_bias, down_bias]), proj_bias])

    start, n1, qkv, mixed, lse, middle, n2, w = attn_fwd(
        n, nz, idx, xs, proj_weight, vec, own_a, own_b, bq, pa, pb)
    *out, mid_grad, mid_low, keep_u, send_u, keep_d, send_d, dub, sums2 = ffn(
        n, nz, idx, gs, n2, middle, up_weight, down_weight, up_bias.reshape(nz, 1, f), vec, fa, fb)
    keep_a, send_a, keep_b, send_b, small, *tok_grad = attn_bwd(
        n, nz, idx, xs, mid_low, mid_grad, start, n1, proj_weight, vec, w, qkv, mixed, lse, sums2, dub)

    up_z, down_z = over_z(fold(keep_u, send_u, False), fold(keep_d, send_d, True))
    output = to_rows(out, BF16)
    up_g, down_g = share(up_z, down_z, (d // n, f // n))

    tokens_grad = to_rows(tok_grad, F32)
    a_z, b_z = over_z(fold(keep_a, send_a, False), fold(keep_b, send_b, True))
    ra = 2 * hw // n
    tail = b_z[ra:]
    b_all = jnp.concatenate([b_z[:ra], tail] + [shift(tail, s) for s in range(1, nz)])
    a_g, b_g, proj_g = share(a_z, b_all, (ra, ra, tail.shape[0]))

    for k in range(nw.bit_length() - 1):
        small = small + swap(small, 1 << k)
    for k in range(nz.bit_length() - 1):
        small = small + lax.ppermute(small, "narrow", [(i, i ^ (1 << k)) for i in range(nz)])
    up_b = lax.dynamic_index_in_dim(small, 8 + me_z, 0, keepdims=False)
    dqv = lax.dynamic_index_in_dim(small, 8 + nz + me_z, 0, keepdims=False)
    qv = jnp.stack([dqv[:hw], dqv[2 * hw:3 * hw]])
    qkv_g = jnp.transpose(a_g.reshape(3, hw, d), (2, 0, 1))
    return (output, tokens_grad, proj_g.reshape(-1, feat, d), small[0:2], small[2], small[3], qkv_g, qv,
            b_g.reshape(hw, d), small[6], small[4], small[5], up_g.reshape(d, f), up_b, down_g.reshape(f, d),
            small[7])


def solution(mesh):
    in_specs = (
        P("wide", "narrow", None), P("wide"), P(), P(), P(), P(), P(None, None, "narrow"),
        P(None, "narrow"), P("narrow", None), P(), P(), P(), P(None, "narrow"), P(),
        P("narrow", None), P(), P("wide", "narrow", None),
    )
    out_specs = (
        P("wide", "narrow", None), P("wide", "narrow", None), P(), P(), P(), P(),
        P(None, None, "narrow"), P(None, "narrow"), P("narrow", None), P(), P(), P(),
        P(None, "narrow"), P("narrow"), P("narrow", None), P(),
    )
    body = functools.partial(per_device, mesh.shape["wide"], mesh.shape["narrow"])

    return jax.shard_map(body, mesh=mesh, in_specs=in_specs, out_specs=out_specs, check_vma=False)
```
